256 devices in a mesh: req: 32 (over x, y, z_lo), tp: 8 (over z_hi, core).
Axes of the slice: x: 4, y: 4, z: 8 (z_hi: 4, z_lo: 2; z = z_hi * 2 + z_lo), core: 2. Of those that a mesh axis runs over, the one named last changes fastest.
Arguments:
- hidden_in: bfloat16 [1024, 24, 3072], P(('req', 'tp')), may hold values from -6 to 6
- norm_gain: float32 [3072], replicated, may hold values from 0.1 to 1.9
- w_q: bfloat16 [3072, 3072], P(None, 'tp'), may hold values from -0.108253175 to 0.108253175
- w_k: bfloat16 [3072, 3072], P(None, 'tp'), may hold values from -3.35584844 to 3.35584844
- w_v: bfloat16 [3072, 3072], P(None, 'tp'), may hold values from -0.109375 to 0.109375
- w_o: bfloat16 [3072, 3072], P('tp'), may hold values from -0.109375 to 0.109375
- lengths: int32 [32, 32], P('req'), may hold values from 1 to 24, 576 in all within a row
- dest: int32 [32, 32, 1], P('req'), may hold values from 0 to 31; in each aligned block of 32 rows (0 to 31, 32 to 63, ..., all dimensions but the last counted through in order) at most 2 rows name the same one
Outputs:
- hidden_out: bfloat16 [1024, 24, 3072], P(('req', 'tp'))
- cache: bfloat16 [2048, 24, 2, 3072], P('req', None, None, 'tp')
The draws below stay inside these ranges and needn't reach their ends.
Inputs may be any that keep to these rules, and one draw needn't show every extreme that they name: Each replica's lengths sum to 576 and the longest is 24. `dest`: no replica names one destination for more than 2 of its requests, and some replica names one exactly 2 times.
All inputs are finite; a program needn't handle non-finite values.
Results may differ from the reference program's by a relative error of at most 0.015.
Values may be sent and summed in bfloat16 or wider, within the bound.
No kernel may reach another device: no remote copies, remote signals or barrier semaphores. Data moves between devices by JAX's collectives and lax.ppermute only.
A program may use at most 128 MiB of HBM per device.

```python
import math
import jax
import jax.numpy as jnp
import numpy as np
from jax import lax

D = 3072
HEADS = 32
HD = 96
SLOT = 24
REQ_REP = 32
CAP = 2
HEADS_DEV = 4
REQUESTS = 1024
CACHE_ROWS = 2048
N_REQ = 32


def shared_base(key):
    return jnp.clip(jax.random.normal(jax.random.fold_in(key, 11), (D, HEADS * HD), jnp.float32), -6.0, 6.0)


def draw_w_q(key, part):
    return (shared_base(key) * D ** (-0.5)).astype(jnp.bfloat16)


def draw_w_k(key, part):
    noise = jnp.clip(jax.random.normal(jax.random.fold_in(key, 12), (D, HEADS * HD), jnp.float32), -6.0, 6.0)
    return (noise * D ** (-0.5)).astype(jnp.bfloat16)


def shard_levels(key, dims, pieces, smallest, high):
    level = 1.0
    for axis_at, shards_of in pieces:
        steps = jax.random.uniform(jax.random.fold_in(jax.random.fold_in(key, 6), axis_at), (shards_of,), jnp.float32, smallest / len(pieces), high / len(pieces))
        level = level * jnp.repeat(jnp.exp(steps), dims[axis_at] // shards_of).reshape((-1,) + (1,) * (len(dims) - 1 - axis_at))
    return level


def split_up(amount, total, most, slope):
    weights = [(1 << 20) // math.isqrt(rank ** slope) + 1 for rank in range(2, amount + 1)]
    spare, holding = total - most - (amount - 1), [1] * (amount - 1)
    while spare > 0:
        free = [i for i in range(amount - 1) if holding[i] < most]
        mass, left = sum([weights[i] for i in free]), spare
        for i in free:
            extra = min(most - holding[i], max(1, left * weights[i] // mass), spare)
            holding[i] = holding[i] + extra
            spare = spare - extra
    return np.array([most] + holding)


def uneven(own_key, number_of, total, reach, lean):
    if number_of == 2:
        one = jax.random.randint(own_key, (), max(1, total - reach), min(reach, total - 1) + 1)
        return jnp.stack([one, total - one])
    sizes = jnp.asarray(split_up(number_of, total, reach, lean), jnp.int32)
    pairs = (number_of - 1) // 2
    donor, taker = sizes[1:1 + 2 * pairs:2], sizes[2:2 + 2 * pairs:2]
    margin = jnp.minimum(donor - 1, reach - taker)
    shifted = jax.random.randint(jax.random.fold_in(own_key, 1), (pairs,), 0, 1 << 20) % (margin + 1)
    sizes = sizes.at[1:1 + 2 * pairs:2].set(donor - shifted).at[2:2 + 2 * pairs:2].set(taker + shifted)
    return sizes[jax.random.permutation(jax.random.fold_in(own_key, 2), number_of)]


def assign_block(own_key, own, number, rows, number_of, top, most, slope):
    sequence = jax.random.permutation(own_key, number_of)
    crowded, common = shares(number_of, rows * top, most, slope, True), shares(number_of, rows * top, most, slope, False)
    places = jnp.arange(number_of)

    def named(tallies, rotation):
        used = int((tallies > 0).sum())
        fixed = max(1, used // 4)
        moved = fixed + (places - fixed + rotation * (used - fixed)) % max(1, number_of - fixed)
        return jnp.zeros((number_of,), jnp.int32).at[sequence[jnp.where(places < fixed, places, moved)]].set(jnp.asarray(tallies, jnp.int32))

    tallies = jnp.where(number % 4 == 0, named(crowded, number // 4), named(common, number - number // 4 - 1))
    mixed = jax.random.permutation(jax.random.fold_in(own, 3), number_of)
    giver, receiver = mixed[0:number_of // 2 * 2:2], mixed[1:number_of // 2 * 2:2]
    slack = jnp.minimum(tallies[giver] - 1, most - tallies[receiver]) // 2
    slack = jnp.where((giver == sequence[0]) | (receiver == sequence[0]) | (tallies[receiver] == 0), 0, jnp.maximum(slack, 0))
    moved = jax.random.randint(jax.random.fold_in(own, 4), (number_of // 2,), 0, 1 << 20) % (slack + 1)
    tallies = tallies.at[giver].add(-moved).at[receiver].add(moved)
    items = jnp.searchsorted(jnp.cumsum(tallies), jnp.arange(rows * top), side="right").astype(jnp.int32)
    listing = items.reshape(top, rows).T
    listing = listing[jax.random.permutation(jax.random.fold_in(own, 1), rows)]
    rotation = jax.random.randint(jax.random.fold_in(own, 2), (rows, 1), 0, top)
    return jnp.take_along_axis(listing, (jnp.arange(top)[None, :] + rotation) % top, axis=1)


def shares(amount, total, bound, skew, full):
    weights = [(1 << 20) // math.isqrt(rank ** skew) + 1 for rank in range(1, amount + 1)]
    largest = bound if full else min(bound, max(-(-total // amount), total * weights[0] // sum(weights)))
    least = 1 if total - largest >= amount - 1 else 0
    given, surplus = [largest] + [least] * (amount - 1), total - largest - least * (amount - 1)
    while surplus > 0:
        candidates = [i for i in range(1, amount) if given[i] < largest] or [i for i in range(1, amount) if given[i] < bound]
        pool, remaining = sum([weights[i] for i in candidates]), surplus
        for i in candidates:
            addition = min(bound - given[i], max(1, remaining * weights[i] // pool), surplus)
            given[i] = given[i] + addition
            surplus = surplus - addition
    return np.array(given)


def bell_draw(own_key, extent, spread, bound, shards=(), kind=jnp.bfloat16):
    gain = shard_levels(own_key, extent, shards, -0.22, 0.18) if shards else 1.0
    values = jax.random.normal(own_key, extent, jnp.float32) * spread * gain
    return jnp.minimum(jnp.maximum(values, -bound), bound).astype(kind)


def setup_inputs(seed: int = 0) -> dict:
    key_list = jax.random.split(jax.random.key(seed), 9)
    hidden_in = bell_draw(key_list[0], (REQUESTS, SLOT, D), 1.0, 6.0, ((0, 256),))
    norm_gain = jnp.clip(1.0 + 0.18 * jax.random.normal(key_list[1], (D,), jnp.float32), 0.1, 1.9)
    w_q = draw_w_q(jax.random.fold_in(key_list[8], 71), 0)
    w_k = draw_w_k(jax.random.fold_in(key_list[8], 71), 0)
    w_v = bell_draw(key_list[4], (D, HEADS * HD), D ** -0.5, 0.109375, ((1, 8),))
    w_o = bell_draw(key_list[5], (HEADS * HD, D), (HEADS * HD) ** -0.5, 0.109375, ((0, 8),))
    lengths = jax.vmap(lambda own: uneven(own, REQ_REP, REQ_REP * SLOT * 3 // 4, SLOT, 2))(jax.random.split(key_list[6], N_REQ)).reshape((N_REQ, REQ_REP)).astype(jnp.int32)
    dest_keys = jax.random.split(jax.random.fold_in(key_list[7], 1), N_REQ * REQ_REP // REQ_REP)
    dest_turns = jax.random.permutation(jax.random.fold_in(key_list[7], 3), N_REQ * REQ_REP // REQ_REP)
    dest = jax.vmap(lambda own, number: assign_block(jax.random.fold_in(key_list[7], 2), own, number, REQ_REP, N_REQ, 1, CAP, 2))(dest_keys, dest_turns).reshape((N_REQ, REQ_REP, 1))
    return {"hidden_in": hidden_in, "norm_gain": norm_gain, "w_q": w_q, "w_k": w_k, "w_v": w_v, "w_o": w_o, "lengths": lengths, "dest": dest}


EPS = 1e-05

def rope_tables():
    pos = jnp.arange(SLOT, dtype=jnp.float32)
    inv = 10000.0 ** (-(jnp.arange(HD // 2, dtype=jnp.float32) * 2.0) / HD)
    angle = pos[:, None] * inv[None, :]
    cosine = jnp.concatenate([jnp.cos(angle), jnp.cos(angle)], -1)
    sine = jnp.concatenate([jnp.sin(angle), jnp.sin(angle)], -1)
    return (cosine, sine)

def rotate(x, cosine, sine):
    half = HD // 2
    turned = jnp.concatenate([-x[..., half:], x[..., :half]], -1)
    return x * cosine[None, :, None, :] + turned * sine[None, :, None, :]

def replica(x, norm_gain, w_q, w_k, w_v, w_o, lens):
    cosine, sine = rope_tables()
    xf = x.astype(jnp.float32)
    mean_sq = lax.optimization_barrier(jnp.mean(xf * xf, -1, keepdims=True))
    normed = (xf * lax.rsqrt(mean_sq + EPS) * norm_gain).astype(jnp.bfloat16)
    flat = normed.reshape(REQ_REP * SLOT, D)
    shape4 = (REQ_REP, SLOT, HEADS, HD)
    query = rotate(jnp.dot(flat, w_q, preferred_element_type=jnp.float32).reshape(shape4), cosine, sine).astype(jnp.bfloat16)
    keys = rotate(jnp.dot(flat, w_k, preferred_element_type=jnp.float32).reshape(shape4), cosine, sine).astype(jnp.bfloat16)
    values = jnp.dot(flat, w_v, preferred_element_type=jnp.float32).astype(jnp.bfloat16).reshape(shape4)
    live = jnp.arange(SLOT, dtype=jnp.int32)[None, :] < lens[:, None]
    causal = jnp.arange(SLOT)[None, :] <= jnp.arange(SLOT)[:, None]
    mask = causal[None, None, :, :] & live[:, None, None, :]
    scores = jnp.einsum('rqhd,rkhd->rhqk', query.astype(jnp.float32), keys.astype(jnp.float32)) / jnp.sqrt(jnp.float32(HD))
    scores = jnp.where(mask, scores, jnp.float32(-1e+30))
    top = lax.optimization_barrier(jnp.max(scores, -1, keepdims=True))
    expo = jnp.where(mask, jnp.exp(scores - top), 0.0)
    probs = (expo / lax.optimization_barrier(jnp.sum(expo, -1, keepdims=True))).astype(jnp.bfloat16)
    attn = jnp.einsum('rhqk,rkhd->rqhd', probs.astype(jnp.float32), values.astype(jnp.float32)).astype(jnp.bfloat16)
    attn = attn.reshape(REQ_REP * SLOT, HEADS * HD)
    group = HEADS_DEV * HD
    summed = jnp.zeros((REQ_REP * SLOT, D), jnp.float32)
    for index in range(HEADS // HEADS_DEV):
        part = jnp.dot(attn[:, index * group:(index + 1) * group], w_o[index * group:(index + 1) * group], preferred_element_type=jnp.float32).astype(jnp.bfloat16)
        part = lax.optimization_barrier(part)
        summed = summed + part.astype(jnp.float32)
    out = (summed + xf.reshape(REQ_REP * SLOT, D)).astype(jnp.bfloat16).reshape(REQ_REP, SLOT, D)
    stacked = jnp.stack([keys, values], 2)
    stacked = jnp.where(live[:, :, None, None, None], stacked, jnp.zeros_like(stacked))
    return (out, stacked.reshape(REQ_REP, SLOT, 2, HEADS * HD))

def reference(hidden_in, norm_gain, w_q, w_k, w_v, w_o, lengths, dest):
    grouped = hidden_in.reshape(N_REQ, REQ_REP, SLOT, D)

    def one(pair):
        return replica(pair[0], norm_gain, w_q, w_k, w_v, w_o, pair[1])
    outs, kvs = lax.map(one, (grouped, lengths))
    hidden_out = outs.reshape(REQUESTS, SLOT, D)
    target = dest[:, :, 0]
    same = target[:, :, None] == target[:, None, :]
    earlier = jnp.arange(REQ_REP)[None, :] < jnp.arange(REQ_REP)[:, None]
    rank = lax.optimization_barrier(jnp.sum((same & earlier[None]).astype(jnp.int32), -1)).astype(jnp.int32)
    source = jnp.arange(N_REQ, dtype=jnp.int32)[:, None]
    rows = (target * (CAP * N_REQ) + source * CAP + rank).astype(jnp.int32)
    cache = jnp.zeros((CACHE_ROWS, SLOT, 2, HEADS * HD), jnp.bfloat16)
    cache = cache.at[rows.reshape(-1)].set(kvs.reshape(REQUESTS, SLOT, 2, HEADS * HD))
    return (hidden_out, cache)
```

```python
import functools

import jax
import jax.numpy as jnp
import numpy as np
from jax import lax
from jax.experimental import pallas as pl
from jax.experimental.pallas import tpu as pltpu
from jax.sharding import Mesh, PartitionSpec as P

HD = 96
CAP = 2
EPS = 1e-05
SLOT = 24
NZ = 8
REQ_REP = 32
REQ_DEV = 4
ROWS = REQ_DEV * SLOT
HALF = ROWS // 2
LANES = 128
VMEM = pl.BlockSpec(memory_space=pltpu.VMEM)
SMEM = pl.BlockSpec(memory_space=pltpu.SMEM)
ANY = pl.BlockSpec(memory_space=pl.ANY)


def rope_tables(width):
    half = HD // 2
    pos = np.arange(SLOT, dtype=np.float32)
    inv = (np.float32(10000.0) ** (-(np.arange(half, dtype=np.float32) * 2.0) / HD)).astype(np.float32)
    angle = pos[:, None] * inv[None, :]
    cosine = np.tile(np.cos(angle), (1, 2 * (width // HD)))
    sine = np.tile(np.concatenate([-np.sin(angle), np.sin(angle)], 1), (1, width // HD))
    return jnp.asarray(cosine, jnp.float32), jnp.asarray(sine, jnp.float32)


def rotate(x, cosine, sine):
    rows, width = x.shape
    lane = lax.broadcasted_iota(jnp.int32, x.shape, 1) % HD
    ahead = pltpu.roll(x, width - HD // 2, 1)
    behind = pltpu.roll(x, HD // 2, 1)
    turned = jnp.where(lane < HD // 2, ahead, behind)
    reps = rows // SLOT
    return x * jnp.concatenate([cosine] * reps, 0) + turned * jnp.concatenate([sine] * reps, 0)


def normed(top, bottom, gain):
    out = []
    for ref in (top, bottom):
        xf = ref[...].astype(jnp.float32)
        mean_sq = jnp.mean(xf * xf, -1, keepdims=True)
        out.append((xf * lax.rsqrt(mean_sq + EPS) * gain).astype(jnp.bfloat16))
    return out


def first_request(meta, back, other_core=0):
    chip = (meta[0] - back + NZ) % NZ
    core = meta[1] if not other_core else 1 - meta[1]
    return (chip % 2) * REQ_REP + ((chip // 2) * 2 + core) * REQ_DEV


def kv_kernel(backs, keep, meta, lens, gain, cosine, sine, wk, wv, wk_p, wv_p, *refs):
    n = len(backs)
    chunks = refs[: 2 * n]
    outs = refs[2 * n :]
    kept = outs[: 2 * len(keep)]
    wire_m, wire_p, x_scr, w_scr = outs[2 * len(keep) :]
    per_dev = wk.shape[1]
    tiles = per_dev // LANES
    rows = n * ROWS
    g = gain[...]
    token = lax.broadcasted_iota(jnp.int32, (SLOT, 1), 0)
    alive = []
    for i, back in enumerate(backs):
        top, bottom = normed(chunks[2 * i], chunks[2 * i + 1], g)
        x_scr[i * ROWS : i * ROWS + HALF, :] = top
        x_scr[i * ROWS + HALF : (i + 1) * ROWS, :] = bottom
        base = first_request(meta, back)
        for j in range(REQ_DEV):
            alive.append((token < lens[base + j]).astype(jnp.float32))
    alive = jnp.concatenate(alive, 0)
    x = x_scr[...]
    for shard, (a, b, wire) in enumerate(((wk, wv, wire_m), (wk_p, wv_p, wire_p))):
        k = jnp.dot(x, a[...], preferred_element_type=jnp.float32)
        k = rotate(k, cosine[...], sine[...]).astype(jnp.bfloat16)
        v = jnp.dot(x, b[...], preferred_element_type=jnp.float32).astype(jnp.bfloat16)
        for s, i in enumerate(keep):
            kept[2 * s][:, shard * per_dev : (shard + 1) * per_dev] = k[i * ROWS : (i + 1) * ROWS]
            kept[2 * s + 1][:, shard * per_dev : (shard + 1) * per_dev] = v[i * ROWS : (i + 1) * ROWS]
        for kv, y in enumerate((k, v)):
            y = y.astype(jnp.float32)
            y = jnp.where(alive > 0.5, y, 0.0)
            for t in range(tiles):
                w_scr[pl.ds(2 * t + kv, rows, stride=2 * tiles), :] = y[:, t * LANES : (t + 1) * LANES]
        wire[...] = w_scr[...].astype(jnp.bfloat16)


def kv_call(backs, keep, meta, lens, gain, cosine, sine, weights, chunks):
    n = len(backs)
    width, per_dev = weights[0].shape
    per_req = SLOT * 2 * per_dev // LANES
    outs = [jax.ShapeDtypeStruct((ROWS, 2 * per_dev), jnp.bfloat16)] * (2 * len(keep))
    outs += [jax.ShapeDtypeStruct((n * REQ_DEV * per_req, LANES), jnp.bfloat16)] * 2
    res = pl.pallas_call(
        functools.partial(kv_kernel, backs, keep),
        out_shape=outs,
        in_specs=[SMEM, SMEM] + [VMEM] * (7 + 2 * n),
        out_specs=[VMEM] * len(outs),
        scratch_shapes=[
            pltpu.VMEM((n * ROWS, width), jnp.bfloat16),
            pltpu.VMEM((n * REQ_DEV * per_req, LANES), jnp.float32),
        ],
        compiler_params=pltpu.CompilerParams(vmem_limit_bytes=40 << 20),
        cost_estimate=pl.CostEstimate(
            flops=2 * n * ROWS * width * 4 * per_dev, bytes_accessed=4 << 20, transcendentals=0
        ),
        name="kv",
    )(meta, lens, gain, cosine, sine, *weights, *chunks)
    wire = [r.reshape(n * REQ_DEV, per_req, LANES) for r in res[-2:]]
    return res[:-2], wire[0], wire[1]


def attn_kernel(back, meta, lens, gain, cosine, sine, wq, wq_p, wo, wo_p, top, bottom, k, v, out, x_scr):
    per_dev = wq.shape[1]
    heads = per_dev // HD
    a, b = normed(top, bottom, gain[...])
    x_scr[:HALF, :] = a
    x_scr[HALF:, :] = b
    base = first_request(meta, back)
    row = lax.broadcasted_iota(jnp.int32, (ROWS, ROWS), 0)
    col = lax.broadcasted_iota(jnp.int32, (ROWS, ROWS), 1)
    limit = jnp.zeros((1, ROWS), jnp.int32)
    which = lax.broadcasted_iota(jnp.int32, (1, ROWS), 1) // SLOT
    for j in range(REQ_DEV):
        limit = jnp.where(which == j, lens[base + j] + j * SLOT, limit)
    mask = (row // SLOT == col // SLOT) & (col <= row) & (col < limit)
    mask = jnp.where(mask, 1.0, 0.0)
    mask = jnp.concatenate([mask] * heads, 0) > 0.5
    head = lax.broadcasted_iota(jnp.int32, (ROWS, per_dev), 1) // HD
    x = x_scr[...]
    parts = []
    for shard, (w, o) in enumerate(((wq, wo), (wq_p, wo_p))):
        q = jnp.dot(x, w[...], preferred_element_type=jnp.float32)
        q = rotate(q, cosine[...], sine[...]).astype(jnp.bfloat16).astype(jnp.float32)
        stacked = jnp.concatenate([jnp.where(head == h, q, 0.0) for h in range(heads)], 0).astype(jnp.bfloat16)
        keys = k[:, shard * per_dev : (shard + 1) * per_dev]
        values = v[:, shard * per_dev : (shard + 1) * per_dev]
        scores = lax.dot_general(
            stacked, keys, (((1,), (1,)), ((), ())), preferred_element_type=jnp.float32
        ) * np.float32(1.0 / np.sqrt(np.float32(HD)))
        scores = jnp.where(mask, scores, -1e30)
        peak = jnp.max(scores, -1, keepdims=True)
        expo = jnp.where(mask, jnp.exp(scores - peak), 0.0)
        probs = (expo / jnp.sum(expo, -1, keepdims=True)).astype(jnp.bfloat16)
        mixed = jnp.dot(probs, values, preferred_element_type=jnp.float32)
        attn = jnp.zeros((ROWS, per_dev), jnp.float32)
        for h in range(heads):
            attn = attn + jnp.where(head == h, mixed[h * ROWS : (h + 1) * ROWS], 0.0)
        parts.append((attn.astype(jnp.bfloat16), o))
    step = 1024
    for at in range(0, out.shape[1], step):
        total = None
        for attn, o in parts:
            y = jnp.dot(attn, o[:, at : at + step], preferred_element_type=jnp.float32)
            total = y if total is None else total + y
        out[:, at : at + step] = total.astype(out.dtype)


def attn_call(back, meta, lens, gain, cosine, sine, weights, chunk, k, v):
    width, per_dev = weights[0].shape
    return pl.pallas_call(
        functools.partial(attn_kernel, back),
        out_shape=jax.ShapeDtypeStruct((ROWS, width), jnp.bfloat16),
        in_specs=[SMEM, SMEM] + [VMEM] * 11,
        out_specs=VMEM,
        scratch_shapes=[pltpu.VMEM((ROWS, width), jnp.bfloat16)],
        compiler_params=pltpu.CompilerParams(vmem_limit_bytes=40 << 20),
        cost_estimate=pl.CostEstimate(
            flops=2 * ROWS * width * 4 * per_dev, bytes_accessed=4 << 20, transcendentals=ROWS * ROWS * 8
        ),
        name="attend",
    )(meta, lens, gain, cosine, sine, *weights, *chunk, k, v)


def pack_kernel(order, meta, slots, empty, *refs):
    wires = refs[: len(order)]
    out, blank, sem = refs[len(order) :]
    blank[...] = jnp.zeros_like(blank)
    for s in range(out.shape[0]):
        @pl.when(empty[s] == 1)
        def _():
            pltpu.make_async_copy(blank, out.at[s], sem).start()
    for (backs, other_core), wire in zip(order, wires):
        for i, back in enumerate(backs):
            base = first_request(meta, back, other_core)
            for j in range(REQ_DEV):
                slot = slots[base + j]

                @pl.when(slot >= 0)
                def _():
                    pltpu.make_async_copy(wire.at[i * REQ_DEV + j], out.at[slot], sem).start()
    pltpu.make_async_copy(out, out, sem).wait()


def pack_call(order, meta, slots, empty, wires):
    per_req = wires[0].shape[1]
    rows = empty.shape[0]
    return pl.pallas_call(
        functools.partial(pack_kernel, order),
        out_shape=jax.ShapeDtypeStruct((rows, per_req, LANES), jnp.bfloat16),
        in_specs=[SMEM] * 3 + [ANY] * len(wires),
        out_specs=ANY,
        scratch_shapes=[pltpu.VMEM((per_req, LANES), jnp.bfloat16), pltpu.SemaphoreType.DMA],
        cost_estimate=pl.CostEstimate(flops=0, bytes_accessed=2 * rows * per_req * LANES * 2, transcendentals=0),
        name="pack",
    )(meta, slots, empty, *wires)


def swap(x, axis):
    return lax.ppermute(x, axis, [(0, 1), (1, 0)])


def shift(x, by):
    at = lambda z: (z % 2) * (NZ // 2) + z // 2
    return lax.ppermute(x, ("zl", "zh"), [(at(z), at((z + by) % NZ)) for z in range(NZ)])


def on_device(hidden_in, norm_gain, w_q, w_k, w_v, w_o, lengths, dest):
    width = hidden_in.shape[-1]
    per_dev = w_q.shape[1]
    zl, zh, core = lax.axis_index("zl"), lax.axis_index("zh"), lax.axis_index("core")
    meta = jnp.stack([zh * 2 + zl, core]).astype(jnp.int32)
    mine = jnp.concatenate([lengths[0], dest[0, :, 0]])
    theirs = swap(mine, "zl")
    both = jnp.where(zl == 0, jnp.stack([mine, theirs]), jnp.stack([theirs, mine]))
    lens = both[:, :REQ_REP].reshape(-1)
    target = both[:, REQ_REP:]
    same = target[:, :, None] == target[:, None, :]
    earlier = jnp.arange(REQ_REP)[None, :] < jnp.arange(REQ_REP)[:, None]
    rank = jnp.sum((same & earlier[None]).astype(jnp.int32), -1)
    slots = (target // 2) * (2 * CAP) + jnp.arange(2)[:, None] * CAP + rank
    slots = jnp.where(target % 2 == zl, slots, -1).reshape(-1)
    out_rows = lax.axis_size("xy") * 2 * CAP
    empty = 1 - jnp.any(slots[None, :] == jnp.arange(out_rows)[:, None], -1).astype(jnp.int32)

    flat = hidden_in.reshape(ROWS, width)
    up = [(flat[:HALF], flat[HALF:])]
    down = [up[0]]
    wk_p, wv_p = swap(w_k, "core"), swap(w_v, "core")
    wq_p, wo_p = swap(w_q, "core"), swap(w_o, "core")
    for _ in range(3):
        a, b = up[-1]
        c, d = down[-1]
        up.append((shift(a, 1), shift(b, 1)))
        down.append((shift(c, -1), shift(d, -1)))
    far = (shift(up[3][0], 1), shift(down[3][1], -1))

    gain = norm_gain.reshape(1, width)
    cosine, sine = rope_tables(per_dev)
    kv_w = (w_k, w_v, wk_p, wv_p)
    at_w = (w_q, wq_p, w_o, wo_p)
    kv = lambda backs, keep, chunks: kv_call(backs, keep, meta, lens, gain, cosine, sine, kv_w, chunks)
    attend = lambda back, chunk, k, v: attn_call(back, meta, lens, gain, cosine, sine, at_w, chunk, k, v)

    order, wires = [], []

    def deliver(backs, own, other):
        order.append((backs, 0))
        wires.append(own)
        order.append((backs, 1))
        wires.append(swap(other, "core"))

    (k0, v0), own, other = kv((0, 1, -1), (0,), up[0] + up[1] + down[1])
    deliver((0, 1, -1), own, other)
    part0 = attend(0, up[0], k0, v0)
    (k1, v1, k2, v2), own, other = kv((2, -2), (0, 1), up[2] + down[2])
    deliver((2, -2), own, other)
    part1 = attend(2, up[2], k1, v1)
    part2 = attend(-2, down[2], k2, v2)
    _, own, other = kv((3, -3), (), up[3] + down[3])
    deliver((3, -3), own, other)
    (k3, v3), own, other = kv((4,), (0,), far)
    deliver((4,), own, other)
    outbound = pack_call(order, meta, slots, empty, wires)
    inbound = lax.all_to_all(outbound, "xy", split_axis=0, concat_axis=0, tiled=True)
    part3 = attend(4, far, k3, v3)
    r1 = shift(part1, -2)
    r2 = shift(part2, 2)
    r3 = shift(part3, 4)
    total = flat.astype(jnp.float32)
    for part in (part0, r1, r2, r3):
        total = total + part.astype(jnp.float32)
    hidden_out = total.astype(jnp.bfloat16).reshape(hidden_in.shape)
    tiles = per_dev // LANES
    cache = inbound.reshape(out_rows, SLOT, tiles, 2, LANES).transpose(0, 1, 3, 2, 4)
    return hidden_out, cache.reshape(out_rows, SLOT, 2, per_dev)


def solution(mesh):
    n_req, n_tp = mesh.devices.shape
    fine = Mesh(mesh.devices.reshape(n_req // 2, 2, n_tp // 2, 2), ("xy", "zl", "zh", "core"))
    req, tp = ("xy", "zl"), ("zh", "core")
    placed = (
        P(req + tp, None, None),
        P(),
        P(None, tp),
        P(None, tp),
        P(None, tp),
        P(tp, None),
        P(req, None),
        P(req, None, None),
    )
    return jax.shard_map(
        on_device,
        mesh=fine,
        in_specs=placed,
        out_specs=(P(req + tp, None, None), P(req, None, None, tp)),
        check_vma=False,
    )
```

```python
import functools

import jax
import jax.numpy as jnp
import numpy as np
from jax import lax
from jax.experimental import pallas as pl
from jax.experimental.pallas import tpu as pltpu
from jax.sharding import Mesh, PartitionSpec as P

HD = 96
CAP = 2
EPS = 1e-05
SLOT = 24
NZ = 8
REQ_REP = 32
REQ_DEV = 4
ROWS = REQ_DEV * SLOT
HALF = ROWS // 2
LANES = 128
VMEM = pl.BlockSpec(memory_space=pltpu.VMEM)
SMEM = pl.BlockSpec(memory_space=pltpu.SMEM)
HBM = pl.BlockSpec(memory_space=pltpu.HBM)


def rope_tables(width):
    half = HD // 2
    pos = np.arange(SLOT, dtype=np.float32)
    inv = (np.float32(10000.0) ** (-(np.arange(half, dtype=np.float32) * 2.0) / HD)).astype(np.float32)
    angle = pos[:, None] * inv[None, :]
    cosine = np.tile(np.cos(angle), (1, 2 * (width // HD)))
    sine = np.tile(np.concatenate([-np.sin(angle), np.sin(angle)], 1), (1, width // HD))
    return jnp.asarray(cosine, jnp.float32), jnp.asarray(sine, jnp.float32)


def rotate(x, cosine, sine):
    rows, width = x.shape
    lane = lax.broadcasted_iota(jnp.int32, x.shape, 1) % HD
    ahead = pltpu.roll(x, width - HD // 2, 1)
    behind = pltpu.roll(x, HD // 2, 1)
    turned = jnp.where(lane < HD // 2, ahead, behind)
    reps = rows // SLOT
    return x * jnp.concatenate([cosine] * reps, 0) + turned * jnp.concatenate([sine] * reps, 0)


def first_request(meta, back, other_core=0):
    chip = (meta[0] - back + NZ) % NZ
    core = meta[1] if not other_core else 1 - meta[1]
    return (chip % 2) * REQ_REP + ((chip // 2) * 2 + core) * REQ_DEV


def load(src, dst, sem):
    pltpu.make_async_copy(src, dst, sem).start()


def landed(dst, sem):
    pltpu.make_async_copy(dst, dst, sem).wait()


def columns(shard, size):
    return pl.ds(pl.multiple_of(shard * size, LANES), size)


def tiled(table, rows):
    return jnp.concatenate([table[...]] * (rows // SLOT), 0)


def score_masks(backs, meta, lens, heads):
    row = lax.broadcasted_iota(jnp.int32, (ROWS, ROWS), 0)
    col = lax.broadcasted_iota(jnp.int32, (ROWS, ROWS), 1)
    causal = (row // SLOT == col // SLOT) & (col <= row)
    which = lax.broadcasted_iota(jnp.int32, (1, ROWS), 1) // SLOT
    masks = []
    for back in backs:
        base = first_request(meta, back)
        limit = jnp.zeros((1, ROWS), jnp.int32)
        for j in range(REQ_DEV):
            limit = jnp.where(which == j, lens[base + j] + j * SLOT, limit)
        mask = jnp.where(causal & (col < limit), 1.0, 0.0)
        masks.append(jnp.concatenate([mask] * heads, 0))
    return masks


def attend_shard(shard, masks, x_scr, k_scr, v_scr, wq_scr, cosine, sine, attn_scr):
    n = len(masks)
    per_dev = wq_scr.shape[-1]
    heads = per_dev // HD
    cols = columns(shard, per_dev)
    head = lax.broadcasted_iota(jnp.int32, (ROWS, per_dev), 1) // HD
    q = jnp.dot(x_scr[: n * ROWS, :], wq_scr[shard], preferred_element_type=jnp.float32)
    q = rotate(q, cosine, sine).astype(jnp.bfloat16).astype(jnp.float32)
    for i in range(n):
        at = slice(i * ROWS, (i + 1) * ROWS)
        qi = q[at]
        stacked = jnp.concatenate([jnp.where(head == h, qi, 0.0) for h in range(heads)], 0)
        scores = lax.dot_general(
            stacked.astype(jnp.bfloat16),
            k_scr[at, cols],
            (((1,), (1,)), ((), ())),
            preferred_element_type=jnp.float32,
        ) * np.float32(1.0 / np.sqrt(np.float32(HD)))
        mask = masks[i] > 0.5
        scores = jnp.where(mask, scores, -1e30)
        peak = jnp.max(scores, -1, keepdims=True)
        expo = jnp.where(mask, jnp.exp(scores - peak), 0.0)
        probs = (expo / jnp.sum(expo, -1, keepdims=True)).astype(jnp.bfloat16)
        y = jnp.dot(probs, v_scr[at, cols], preferred_element_type=jnp.float32)
        attn = jnp.where(head == 0, y[:ROWS], 0.0)
        for h in range(1, heads):
            attn = jnp.where(head == h, y[h * ROWS : (h + 1) * ROWS], attn)
        attn_scr[at, cols] = attn.astype(jnp.bfloat16)


def project(attn_scr, wo_scr, part_scr, outs, sems):
    width = wo_scr.shape[1]
    step = 768

    def body(c, carry):
        cols = columns(c, step)
        y = jnp.dot(attn_scr[...], wo_scr[:, cols], preferred_element_type=jnp.float32)
        part_scr[:, cols] = y.astype(jnp.bfloat16)
        return carry

    lax.fori_loop(0, width // step, body, 0)
    for i, out in enumerate(outs):
        load(part_scr.at[pl.ds(i * HALF, HALF)], out, sems.at[i])


def load_weights(shard, sources, held, sems):
    wk, wv, wq, wo = sources
    wkv_v, wq_v, wo_v = held
    per_dev = wk.shape[1]
    load(wk, wkv_v.at[shard, :, pl.ds(0, per_dev)], sems.at[shard, 0])
    load(wv, wkv_v.at[shard, :, pl.ds(per_dev, per_dev)], sems.at[shard, 1])
    load(wq, wq_v.at[shard], sems.at[shard, 2])
    load(wo, wo_v.at[pl.ds(shard * per_dev, per_dev)], sems.at[shard, 3])


def held_shapes(width, per_dev):
    return [
        pltpu.VMEM((2, width, 2 * per_dev), jnp.bfloat16),
        pltpu.VMEM((2, width, per_dev), jnp.bfloat16),
        pltpu.VMEM((2 * per_dev, width), jnp.bfloat16),
    ]


def pinned(held):
    return [pltpu.with_memory_space_constraint(w, pltpu.VMEM) for w in held]


def kv_kernel(backs, n_att, pieces, fill, *refs):
    refs = list(refs)
    take = lambda count: [refs.pop(0) for _ in range(count)]
    meta, lens, gain, cosine, sine = take(5)
    weights = take(8 if fill else 3)
    chunks = take(pieces)
    wkv_v, wq_v, wo_v = take(3) if fill else weights
    parts = take(2 * n_att)
    wires = take(2)
    g_scr, cos_scr, sin_scr, x_scr, w_scr, wire_scr, small, piece_sem, w_sem, out_sem = take(10)
    if n_att:
        k_scr, v_scr = take(2)
        attn_scr, part_scr, part_sem = take(3)
    per_dev = wq_v.shape[2]
    tiles = per_dev // LANES
    rows = len(backs) * ROWS
    load(gain, g_scr, small.at[0])
    spans, at = [], 0
    for i, ref in enumerate(chunks):
        spans.append(pl.ds(at, ref.shape[0]))
        load(ref, x_scr.at[spans[-1]], piece_sem.at[i])
        at += ref.shape[0]
    load(cosine, cos_scr, small.at[1])
    load(sine, sin_scr, small.at[2])
    if fill:
        load_weights(0, weights[:4], (wkv_v, wq_v, wo_v), w_sem)
        load_weights(1, weights[4:], (wkv_v, wq_v, wo_v), w_sem)
    token = lax.broadcasted_iota(jnp.int32, (SLOT, 1), 0)
    alive = []
    for back in backs:
        base = first_request(meta, back)
        for j in range(REQ_DEV):
            alive.append((token < lens[base + j]).astype(jnp.float32))
    alive = jnp.concatenate(alive, 0)
    masks = score_masks(backs[:n_att], meta, lens, per_dev // HD) if n_att else []
    landed(g_scr, small.at[0])
    for i, span in enumerate(spans):
        landed(x_scr.at[span], piece_sem.at[i])
        xf = x_scr[span, :].astype(jnp.float32)
        mean_sq = jnp.mean(xf * xf, -1, keepdims=True)
        x_scr[span, :] = (xf * lax.rsqrt(mean_sq + EPS) * g_scr[...]).astype(jnp.bfloat16)
    landed(cos_scr, small.at[1])
    landed(sin_scr, small.at[2])

    def body(shard, carry):
        cols = columns(shard, per_dev)
        if fill:
            landed(wkv_v.at[shard, :, pl.ds(0, per_dev)], w_sem.at[shard, 0])
            landed(wkv_v.at[shard, :, pl.ds(per_dev, per_dev)], w_sem.at[shard, 1])
        y = jnp.dot(x_scr[...], wkv_v[shard], preferred_element_type=jnp.float32)
        k = rotate(y[:, :per_dev], cos_scr[...], sin_scr[...]).astype(jnp.bfloat16)
        v = y[:, per_dev:].astype(jnp.bfloat16)
        if n_att:
            k_scr[:, cols] = k[: k_scr.shape[0]]
            v_scr[:, cols] = v[: v_scr.shape[0]]
        for kv, y in enumerate((k, v)):
            y = jnp.where(alive > 0.5, y.astype(jnp.float32), 0.0)
            for t in range(tiles):
                w_scr[pl.ds(2 * t + kv, rows, stride=2 * tiles), :] = y[:, t * LANES : (t + 1) * LANES]
        wire_scr[shard] = w_scr[...].astype(jnp.bfloat16)
        for i, wire in enumerate(wires):

            @pl.when(shard == i)
            def _():
                load(wire_scr.at[i], wire, out_sem.at[i])

        if fill:
            landed(wq_v.at[shard], w_sem.at[shard, 2])
        if n_att:
            attend_shard(shard, masks, x_scr, k_scr, v_scr, wq_v, cos_scr[...], sin_scr[...], attn_scr)
        return carry

    lax.fori_loop(0, 2, body, 0)
    if fill:
        landed(wo_v.at[pl.ds(0, per_dev)], w_sem.at[0, 3])
        landed(wo_v.at[pl.ds(per_dev, per_dev)], w_sem.at[1, 3])
    if n_att:
        project(attn_scr, wo_v, part_scr, parts, part_sem)
        for i, part in enumerate(parts):
            landed(part, part_sem.at[i])
    for i, wire in enumerate(wires):
        landed(wire, out_sem.at[i])


def kv_call(backs, n_att, meta, lens, tables, weights, chunks):
    n = len(backs)
    fill = len(weights) == 8
    width, per_dev = weights[0].shape if fill else weights[1].shape[1:]
    per_req = SLOT * 2 * per_dev // LANES
    bf16 = lambda *shape: jax.ShapeDtypeStruct(shape, jnp.bfloat16)
    scr = lambda *shape: pltpu.VMEM(shape, jnp.bfloat16)
    outs = (held_shapes(width, per_dev) if fill else []) + [bf16(HALF, width)] * (2 * n_att)
    outs += [bf16(n * REQ_DEV * per_req, LANES)] * 2
    dma = pltpu.SemaphoreType.DMA
    scratch = [pltpu.VMEM(y.shape, y.dtype) for y in tables]
    scratch += [
        scr(n * ROWS, width),
        pltpu.VMEM((n * REQ_DEV * per_req, LANES), jnp.float32),
        scr(2, n * REQ_DEV * per_req, LANES),
        dma((3,)),
        dma((len(chunks),)),
        dma((2, 4)),
        dma((2,)),
    ]
    if n_att:
        scratch += [scr(n_att * ROWS, 2 * per_dev)] * 3 + [scr(n_att * ROWS, width), dma((2 * n_att,))]
    res = pl.pallas_call(
        functools.partial(kv_kernel, backs, n_att, len(chunks), fill),
        out_shape=outs,
        in_specs=[SMEM, SMEM] + [HBM] * 3 + ([HBM] * 8 if fill else [VMEM] * 3) + [HBM] * len(chunks),
        out_specs=[VMEM] * (3 * fill) + [HBM] * (len(outs) - 3 * fill),
        scratch_shapes=scratch,
        compiler_params=pltpu.CompilerParams(vmem_limit_bytes=24 << 20),
        cost_estimate=pl.CostEstimate(
            flops=(n + n_att) * ROWS * width * per_dev // 4, bytes_accessed=1 << 18, transcendentals=0
        ),
        name="keys",
    )(meta, lens, *tables, *(weights if fill else pinned(weights)), *chunks)
    wire = [r.reshape(n * REQ_DEV, per_req, LANES) for r in res[-2:]]
    return res[:-2], wire[0], wire[1]


def pack_kernel(order, meta, slots, empty, *refs):
    sources = refs[: len(order)]
    out, *wires, blank, sem, in_sem = refs[len(order) :]
    for i, (src, dst) in enumerate(zip(sources, wires)):
        load(src, dst, in_sem.at[i])
    blank[...] = jnp.zeros_like(blank)
    for s in range(out.shape[0]):

        @pl.when(empty[s] == 1)
        def _():
            pltpu.make_async_copy(blank, out.at[s], sem).start()

    for w, ((backs, other_core), wire) in enumerate(zip(order, wires)):
        landed(wire, in_sem.at[w])
        for i, back in enumerate(backs):
            base = first_request(meta, back, other_core)
            for j in range(REQ_DEV):
                slot = slots[base + j]

                @pl.when(slot >= 0)
                def _():
                    pltpu.make_async_copy(wire.at[i * REQ_DEV + j], out.at[slot], sem).start()

    pltpu.make_async_copy(out, out, sem).wait()


def pack_call(order, meta, slots, empty, wires):
    per_req = wires[0].shape[1]
    rows = empty.shape[0]
    return pl.pallas_call(
        functools.partial(pack_kernel, order),
        out_shape=jax.ShapeDtypeStruct((rows, per_req, LANES), jnp.bfloat16),
        in_specs=[SMEM] * 3 + [HBM] * len(wires),
        out_specs=HBM,
        scratch_shapes=[pltpu.VMEM(w.shape, w.dtype) for w in wires]
        + [pltpu.VMEM((per_req, LANES), jnp.bfloat16), pltpu.SemaphoreType.DMA]
        + [pltpu.SemaphoreType.DMA((len(wires),))],
        compiler_params=pltpu.CompilerParams(vmem_limit_bytes=24 << 20),
        cost_estimate=pl.CostEstimate(flops=0, bytes_accessed=1 << 18, transcendentals=0),
        name="pack",
    )(meta, slots, empty, *wires)


def place_kernel(wire, out, sem):
    copies = []
    for t in range(wire.shape[2]):
        copies.append(
            pltpu.make_async_copy(wire.at[:, :, t], out.at[:, :, :, pl.ds(t * LANES, LANES)], sem.at[t])
        )
        copies[-1].start()
    for copy in copies:
        copy.wait()


def place_call(inbound, per_dev):
    rows = inbound.shape[0]
    tiles = per_dev // LANES
    wire = inbound.reshape(rows, SLOT, tiles, 2, LANES)
    return pl.pallas_call(
        place_kernel,
        out_shape=jax.ShapeDtypeStruct((rows, SLOT, 2, per_dev), jnp.bfloat16),
        in_specs=[VMEM],
        out_specs=HBM,
        scratch_shapes=[pltpu.SemaphoreType.DMA((tiles,))],
        compiler_params=pltpu.CompilerParams(vmem_limit_bytes=8 << 20),
        name="place",
    )(wire)


def swap(x, axis):
    return lax.ppermute(x, axis, [(0, 1), (1, 0)])


def shift(x, by):
    at = lambda z: (z % 2) * (NZ // 2) + z // 2
    return lax.ppermute(x, ("zl", "zh"), [(at(z), at((z + by) % NZ)) for z in range(NZ)])


def on_device(hidden_in, norm_gain, w_q, w_k, w_v, w_o, lengths, dest):
    width = hidden_in.shape[-1]
    per_dev = w_q.shape[1]
    zl, zh, core = lax.axis_index("zl"), lax.axis_index("zh"), lax.axis_index("core")
    meta = jnp.stack([zh * 2 + zl, core]).astype(jnp.int32)
    mine = jnp.concatenate([lengths[0], dest[0, :, 0]])
    theirs = swap(mine, "zl")
    both = jnp.where(zl == 0, jnp.stack([mine, theirs]), jnp.stack([theirs, mine]))
    lens = both[:, :REQ_REP].reshape(-1)
    target = both[:, REQ_REP:]
    same = target[:, :, None] == target[:, None, :]
    earlier = jnp.arange(REQ_REP)[None, :] < jnp.arange(REQ_REP)[:, None]
    rank = jnp.sum((same & earlier[None]).astype(jnp.int32), -1)
    slots = (target // 2) * (2 * CAP) + jnp.arange(2)[:, None] * CAP + rank
    slots = jnp.where(target % 2 == zl, slots, -1).reshape(-1)
    out_rows = lax.axis_size("xy") * 2 * CAP
    empty = 1 - jnp.any(slots[None, :] == jnp.arange(out_rows)[:, None], -1).astype(jnp.int32)

    flat = hidden_in.reshape(ROWS, width)
    bar = lax.optimization_barrier
    tables = (norm_gain.reshape(1, width), *rope_tables(per_dev))
    order, wires = [], []

    def keys(backs, n_att, weights, chunks):
        extra, own, other = kv_call(backs, n_att, meta, lens, tables, weights, chunks)
        order.append((backs, 0))
        wires.append(own)
        order.append((backs, 1))
        wires.append(swap(other, "core"))
        return extra, own

    u1, d1 = shift(flat, 1), shift(flat, -1)
    wk_p, wv_p = swap(w_k, "core"), swap(w_v, "core")
    wk_p, wq_late, wo_late = bar((wk_p, w_q, w_o))
    u1, d1, meta, lens, slots, empty = bar((u1, d1, meta, lens, slots, empty))
    u2, d2 = shift(u1, 1), shift(d1, -1)
    wq_p, wo_p = swap(wq_late, "core"), swap(wo_late, "core")
    weights = (w_k, w_v, w_q, w_o, wk_p, wv_p, wq_p, wo_p)
    extra, done = keys((0, 1, -1), 1, weights, (flat, u1, d1))
    held, part0 = extra[:3], extra[3:]
    u2, d2, done = bar((u2, d2, done))
    wires[0] = done
    u3, d3 = shift(u2, 1), shift(d2, -1)
    (top1, bottom1, top2, bottom2), done = keys((2, -2), 2, held, (u2, d2))
    u3, d3, done = bar((u3, d3, done))
    wires[2] = done
    far = shift(u3[:HALF], 1), shift(d3[HALF:], -1)
    _, done = keys((3, -3), 0, held, (u3, d3))
    wires[4] = done
    near_t, near_b = shift(top1, -2), shift(bottom2, 2)
    (top3, bottom3), _ = keys((4,), 1, held, far)
    passing_t, passing_b = shift(top3, 2), shift(bottom3, -2)
    outbound = pack_call(order, meta, slots, empty, wires)
    inbound = lax.all_to_all(outbound, "xy", split_axis=0, concat_axis=0, tiled=True)
    add = lambda *ys: sum(y.astype(jnp.float32) for y in ys)
    merged_t = shift(add(top2, passing_t).astype(jnp.bfloat16), 2)
    merged_b = shift(add(bottom1, passing_b).astype(jnp.bfloat16), -2)
    top = add(flat[:HALF], part0[0], near_t, merged_t)
    bottom = add(flat[HALF:], part0[1], near_b, merged_b)
    hidden_out = jnp.concatenate([top, bottom]).astype(jnp.bfloat16).reshape(hidden_in.shape)
    return hidden_out, place_call(inbound, per_dev)


def solution(mesh):
    n_req, n_tp = mesh.devices.shape
    fine = Mesh(mesh.devices.reshape(n_req // 2, 2, n_tp // 2, 2), ("xy", "zl", "zh", "core"))
    req, tp = ("xy", "zl"), ("zh", "core")
    placed = (
        P(req + tp, None, None),
        P(),
        P(None, tp),
        P(None, tp),
        P(None, tp),
        P(tp, None),
        P(req, None),
        P(req, None, None),
    )
    return jax.shard_map(
        on_device,
        mesh=fine,
        in_specs=placed,
        out_specs=(P(req + tp, None, None), P(req, None, None, tp)),
        check_vma=False,
    )
```

```python
import functools

import jax
import jax.numpy as jnp
import numpy as np
from jax import lax
from jax.experimental import pallas as pl
from jax.experimental.pallas import tpu as pltpu
from jax.sharding import Mesh, PartitionSpec as P

HD = 96
CAP = 2
EPS = 1e-05
SLOT = 24
NZ = 8
REQ_REP = 32
REQ_DEV = 4
ROWS = REQ_DEV * SLOT
HALF = ROWS // 2
LANES = 128
MERGE_FLOPS = 3 * 10**10
VMEM = pl.BlockSpec(memory_space=pltpu.VMEM)
SMEM = pl.BlockSpec(memory_space=pltpu.SMEM)
HBM = pl.BlockSpec(memory_space=pltpu.HBM)


def rope_tables(width):
    half = HD // 2
    pos = np.arange(SLOT, dtype=np.float32)
    inv = (np.float32(10000.0) ** (-(np.arange(half, dtype=np.float32) * 2.0) / HD)).astype(np.float32)
    angle = pos[:, None] * inv[None, :]
    cosine = np.tile(np.cos(angle), (1, 2 * (width // HD)))
    sine = np.tile(np.concatenate([-np.sin(angle), np.sin(angle)], 1), (1, width // HD))
    return jnp.asarray(cosine, jnp.float32), jnp.asarray(sine, jnp.float32)


def rotate(x, cosine, sine):
    rows, width = x.shape
    lane = lax.broadcasted_iota(jnp.int32, x.shape, 1) % HD
    ahead = pltpu.roll(x, width - HD // 2, 1)
    behind = pltpu.roll(x, HD // 2, 1)
    turned = jnp.where(lane < HD // 2, ahead, behind)
    reps = rows // SLOT
    return x * jnp.concatenate([cosine] * reps, 0) + turned * jnp.concatenate([sine] * reps, 0)


def first_request(meta, back, other_core=0):
    chip = (meta[0] - back + NZ) % NZ
    core = meta[1] if not other_core else 1 - meta[1]
    return (chip % 2) * REQ_REP + ((chip // 2) * 2 + core) * REQ_DEV


def load(src, dst, sem):
    pltpu.make_async_copy(src, dst, sem).start()


def landed(dst, sem):
    pltpu.make_async_copy(dst, dst, sem).wait()


def columns(shard, size):
    return pl.ds(pl.multiple_of(shard * size, LANES), size)


def tiled(table, rows):
    return jnp.concatenate([table[...]] * (rows // SLOT), 0)


def score_masks(backs, meta, lens, heads):
    row = lax.broadcasted_iota(jnp.int32, (ROWS, ROWS), 0)
    col = lax.broadcasted_iota(jnp.int32, (ROWS, ROWS), 1)
    causal = (row // SLOT == col // SLOT) & (col <= row)
    which = lax.broadcasted_iota(jnp.int32, (1, ROWS), 1) // SLOT
    masks = []
    for back in backs:
        base = first_request(meta, back)
        limit = jnp.zeros((1, ROWS), jnp.int32)
        for j in range(REQ_DEV):
            limit = jnp.where(which == j, lens[base + j] + j * SLOT, limit)
        mask = jnp.where(causal & (col < limit), 1.0, 0.0)
        masks.append(jnp.concatenate([mask] * heads, 0))
    return masks


def attend_shard(shard, masks, x_scr, k_scr, v_scr, wq_scr, cosine, sine, attn_scr):
    n = len(masks)
    per_dev = wq_scr.shape[-1]
    heads = per_dev // HD
    cols = columns(shard, per_dev)
    head = lax.broadcasted_iota(jnp.int32, (ROWS, per_dev), 1) // HD
    q = jnp.dot(x_scr[: n * ROWS, :], wq_scr[shard], preferred_element_type=jnp.float32)
    q = rotate(q, cosine, sine).astype(jnp.bfloat16).astype(jnp.float32)
    for i in range(n):
        at = slice(i * ROWS, (i + 1) * ROWS)
        qi = q[at]
        stacked = jnp.concatenate([jnp.where(head == h, qi, 0.0) for h in range(heads)], 0)
        scores = lax.dot_general(
            stacked.astype(jnp.bfloat16),
            k_scr[at, cols],
            (((1,), (1,)), ((), ())),
            preferred_element_type=jnp.float32,
        ) * np.float32(1.0 / np.sqrt(np.float32(HD)))
        mask = masks[i] > 0.5
        scores = jnp.where(mask, scores, -1e30)
        peak = jnp.max(scores, -1, keepdims=True)
        expo = jnp.where(mask, jnp.exp(scores - peak), 0.0)
        probs = (expo / jnp.sum(expo, -1, keepdims=True)).astype(jnp.bfloat16)
        y = jnp.dot(probs, v_scr[at, cols], preferred_element_type=jnp.float32)
        attn = jnp.where(head == 0, y[:ROWS], 0.0)
        for h in range(1, heads):
            attn = jnp.where(head == h, y[h * ROWS : (h + 1) * ROWS], attn)
        attn_scr[at, cols] = attn.astype(jnp.bfloat16)


def project(attn_scr, wo_scr, part_scr, outs, sems):
    width = wo_scr.shape[1]
    step = 768

    def body(c, carry):
        cols = columns(c, step)
        y = jnp.dot(attn_scr[...], wo_scr[:, cols], preferred_element_type=jnp.float32)
        part_scr[:, cols] = y.astype(jnp.bfloat16)
        return carry

    lax.fori_loop(0, width // step, body, 0)
    for i, out in enumerate(outs):
        load(part_scr.at[pl.ds(i * HALF, HALF)], out, sems.at[i])


def load_keys(weights, wkv_v, sems):
    per_dev = weights[0].shape[1]
    for i, w in enumerate(weights):
        load(w, wkv_v.at[i // 2, :, pl.ds(i % 2 * per_dev, per_dev)], sems.at[i])


def load_rest(weights, wq_v, wo_v, sems):
    wq, wq_p, wo, wo_p = weights
    per_dev = wq.shape[1]
    load(wq, wq_v.at[0], sems.at[0])
    load(wq_p, wq_v.at[1], sems.at[1])
    load(wo, wo_v.at[pl.ds(0, per_dev)], sems.at[2])
    load(wo_p, wo_v.at[pl.ds(per_dev, per_dev)], sems.at[3])


def rest_landed(wo_v, per_dev, sems):
    landed(wo_v.at[pl.ds(0, per_dev)], sems.at[2])
    landed(wo_v.at[pl.ds(per_dev, per_dev)], sems.at[3])


def held_shapes(width, per_dev):
    return [
        pltpu.VMEM((2, width, 2 * per_dev), jnp.bfloat16),
        pltpu.VMEM((2, width, per_dev), jnp.bfloat16),
        pltpu.VMEM((2 * per_dev, width), jnp.bfloat16),
    ]


def pinned(held, space=pltpu.VMEM):
    return [pltpu.with_memory_space_constraint(w, space) for w in held]


def kv_kernel(backs, att, keep, pieces, fill, *refs):
    refs = list(refs)
    take = lambda count: [refs.pop(0) for _ in range(count)]
    fill_keys, fill_rest = fill
    n_att = len(att)
    extra = n_att - len(backs) if n_att else 0
    meta, lens, gain, cosine, sine = take(5)
    key_w = take(4 if fill_keys else 1)
    rest_w = take((4 if fill_rest else 2) if n_att else 0)
    chunks = take(pieces)
    given = take(3 if extra else 0)
    (wkv_v,) = take(1) if fill_keys else key_w
    if n_att:
        wq_v, wo_v = take(2) if fill_rest else rest_w
    parts = take(2 * n_att)
    kept = take(3 if keep else 0)
    wires = take(2)
    g_scr, cos_scr, sin_scr, x_scr, w_scr, wire_scr, small, piece_sem, key_sem, rest_sem, out_sem, given_sem = take(
        12
    )
    if n_att or keep:
        k_scr, v_scr = take(2)
    if n_att:
        attn_scr, part_scr, part_sem = take(3)
    per_dev = wkv_v.shape[2] // 2
    tiles = per_dev // LANES
    rows = len(backs) * ROWS
    load(gain, g_scr, small.at[0])
    spans, at = [], 0
    for i, ref in enumerate(chunks):
        spans.append(pl.ds(at, ref.shape[0]))
        load(ref, x_scr.at[spans[-1]], piece_sem.at[i])
        at += ref.shape[0]
    load(cosine, cos_scr, small.at[1])
    load(sine, sin_scr, small.at[2])
    handed = []
    if extra:
        late = pl.ds(rows, ROWS)
        handed = [x_scr.at[late], k_scr.at[late], v_scr.at[late]]
        for i, (src, dst) in enumerate(zip(given, handed)):
            load(src, dst, given_sem.at[i])
    if fill_keys:
        load_keys(key_w, wkv_v, key_sem)
    if fill_rest:
        load_rest(rest_w, wq_v, wo_v, rest_sem)
    token = lax.broadcasted_iota(jnp.int32, (SLOT, 1), 0)
    alive = []
    for back in backs:
        base = first_request(meta, back)
        for j in range(REQ_DEV):
            alive.append((token < lens[base + j]).astype(jnp.float32))
    alive = jnp.concatenate(alive, 0)
    masks = score_masks(att, meta, lens, per_dev // HD) if n_att else []
    landed(g_scr, small.at[0])
    for i, span in enumerate(spans):
        landed(x_scr.at[span], piece_sem.at[i])
        xf = x_scr[span, :].astype(jnp.float32)
        mean_sq = jnp.mean(xf * xf, -1, keepdims=True)
        x_scr[span, :] = (xf * lax.rsqrt(mean_sq + EPS) * g_scr[...]).astype(jnp.bfloat16)
    landed(cos_scr, small.at[1])
    landed(sin_scr, small.at[2])
    for i, y in enumerate(handed):
        landed(y, given_sem.at[i])
    if keep:
        load(x_scr.at[pl.ds(0, keep * ROWS)], kept[0], small.at[0])

    def body(shard, carry):
        cols = columns(shard, per_dev)
        if fill_keys:
            for i in range(2):
                landed(wkv_v.at[shard, :, pl.ds(i * per_dev, per_dev)], key_sem.at[2 * shard + i])
        y = jnp.dot(x_scr[:rows, :], wkv_v[shard], preferred_element_type=jnp.float32)
        k = rotate(y[:, :per_dev], cos_scr[...], sin_scr[...]).astype(jnp.bfloat16)
        v = y[:, per_dev:].astype(jnp.bfloat16)
        if n_att or keep:
            count = rows if n_att else keep * ROWS
            k_scr[:count, cols] = k[:count]
            v_scr[:count, cols] = v[:count]
        for kv, y in enumerate((k, v)):
            y = jnp.where(alive > 0.5, y.astype(jnp.float32), 0.0)
            for t in range(tiles):
                w_scr[pl.ds(2 * t + kv, rows, stride=2 * tiles), :] = y[:, t * LANES : (t + 1) * LANES]
        wire_scr[shard] = w_scr[...].astype(jnp.bfloat16)
        for i, wire in enumerate(wires):

            @pl.when(shard == i)
            def _():
                load(wire_scr.at[i], wire, out_sem.at[i])

        if fill_rest:
            landed(wq_v.at[shard], rest_sem.at[shard])
        if n_att:
            attend_shard(shard, masks, x_scr, k_scr, v_scr, wq_v, cos_scr[...], sin_scr[...], attn_scr)
        return carry

    lax.fori_loop(0, 2, body, 0)
    if keep:
        load(k_scr, kept[1], small.at[1])
        load(v_scr, kept[2], small.at[2])
    if fill_rest:
        rest_landed(wo_v, per_dev, rest_sem)
    if n_att:
        project(attn_scr, wo_v, part_scr, parts, part_sem)
        for i, part in enumerate(parts):
            landed(part, part_sem.at[i])
    for i, wire in enumerate(wires):
        landed(wire, out_sem.at[i])
    for i, y in enumerate(kept):
        landed(y, small.at[i])


def kv_call(backs, att, keep, meta, lens, tables, key_w, rest_w, chunks, given):
    n = len(backs)
    n_att = len(att)
    fill = (len(key_w) == 4, n_att > 0 and len(rest_w) == 4)
    width, per_dev = key_w[0].shape if fill[0] else (key_w[0].shape[1], key_w[0].shape[2] // 2)
    per_req = SLOT * 2 * per_dev // LANES
    bf16 = lambda *shape: jax.ShapeDtypeStruct(shape, jnp.bfloat16)
    scr = lambda *shape: pltpu.VMEM(shape, jnp.bfloat16)
    held = held_shapes(width, per_dev)
    outs = held[:1] * fill[0] + held[1:] * fill[1]
    n_held = len(outs)
    outs += [bf16(HALF, width)] * (2 * n_att)
    if keep:
        outs += [bf16(keep * ROWS, width)] + [bf16(keep * ROWS, 2 * per_dev)] * 2
    outs += [bf16(n * REQ_DEV * per_req, LANES)] * 2
    dma = pltpu.SemaphoreType.DMA
    scratch = [pltpu.VMEM(y.shape, y.dtype) for y in tables]
    scratch += [
        scr(max(n, n_att) * ROWS, width),
        pltpu.VMEM((n * REQ_DEV * per_req, LANES), jnp.float32),
        scr(2, n * REQ_DEV * per_req, LANES),
        dma((3,)),
        dma((len(chunks),)),
        dma((4,)),
        dma((4,)),
        dma((2,)),
        dma((3,)),
    ]
    local = max(n_att, keep)
    if local:
        scratch += [scr(local * ROWS, 2 * per_dev)] * 2
    if n_att:
        scratch += [scr(n_att * ROWS, 2 * per_dev), scr(n_att * ROWS, width), dma((2 * n_att,))]
    key_w = key_w if fill[0] else pinned(key_w)
    rest_w = rest_w if fill[1] else pinned(rest_w) if n_att else []
    res = pl.pallas_call(
        functools.partial(kv_kernel, backs, att, keep, len(chunks), fill),
        out_shape=outs,
        in_specs=[SMEM, SMEM]
        + [HBM] * 3
        + [HBM if fill[0] else VMEM] * len(key_w)
        + [HBM if fill[1] else VMEM] * len(rest_w)
        + [HBM] * (len(chunks) + len(given)),
        out_specs=[VMEM] * n_held + [HBM] * (len(outs) - n_held),
        scratch_shapes=scratch,
        compiler_params=pltpu.CompilerParams(vmem_limit_bytes=24 << 20),
        cost_estimate=pl.CostEstimate(
            flops=(n + n_att) * ROWS * width * per_dev // 4, bytes_accessed=1 << 18, transcendentals=0
        ),
        name="keys",
    )(meta, lens, *pinned(tables, pltpu.HBM), *key_w, *rest_w, *chunks, *given)
    wire = [r.reshape(n * REQ_DEV, per_req, LANES) for r in res[-2:]]
    return res[:-2], wire[0], wire[1]


def pack_kernel(order, meta, slots, empty, *refs):
    sources = refs[: len(order)]
    out, *wires, blank, sem, in_sem = refs[len(order) :]
    for i, (src, dst) in enumerate(zip(sources, wires)):
        load(src, dst, in_sem.at[i])
    blank[...] = jnp.zeros_like(blank)
    for s in range(out.shape[0]):

        @pl.when(empty[s] == 1)
        def _():
            pltpu.make_async_copy(blank, out.at[s], sem).start()

    for w, ((backs, other_core), wire) in enumerate(zip(order, wires)):
        landed(wire, in_sem.at[w])
        for i, back in enumerate(backs):
            base = first_request(meta, back, other_core)
            for j in range(REQ_DEV):
                slot = slots[base + j]

                @pl.when(slot >= 0)
                def _():
                    pltpu.make_async_copy(wire.at[i * REQ_DEV + j], out.at[slot], sem).start()

    pltpu.make_async_copy(out, out, sem).wait()


def pack_call(order, meta, slots, empty, wires):
    per_req = wires[0].shape[1]
    rows = empty.shape[0]
    return pl.pallas_call(
        functools.partial(pack_kernel, order),
        out_shape=pltpu.HBM((rows, per_req, LANES), jnp.bfloat16),
        in_specs=[SMEM] * 3 + [HBM] * len(wires),
        out_specs=HBM,
        scratch_shapes=[pltpu.VMEM(w.shape, w.dtype) for w in wires]
        + [pltpu.VMEM((per_req, LANES), jnp.bfloat16), pltpu.SemaphoreType.DMA]
        + [pltpu.SemaphoreType.DMA((len(wires),))],
        compiler_params=pltpu.CompilerParams(vmem_limit_bytes=24 << 20),
        cost_estimate=pl.CostEstimate(flops=0, bytes_accessed=1 << 18, transcendentals=0),
        name="pack",
    )(meta, slots, empty, *wires)


def place_kernel(wire, out, sem):
    copies = []
    for t in range(wire.shape[2]):
        copies.append(
            pltpu.make_async_copy(wire.at[:, :, t], out.at[:, :, :, pl.ds(t * LANES, LANES)], sem.at[t])
        )
        copies[-1].start()
    for copy in copies:
        copy.wait()


def place_call(inbound, per_dev):
    rows = inbound.shape[0]
    tiles = per_dev // LANES
    wire = inbound.reshape(rows, SLOT, tiles, 2, LANES)
    return pl.pallas_call(
        place_kernel,
        out_shape=jax.ShapeDtypeStruct((rows, SLOT, 2, per_dev), jnp.bfloat16),
        in_specs=[VMEM],
        out_specs=HBM,
        scratch_shapes=[pltpu.SemaphoreType.DMA((tiles,))],
        compiler_params=pltpu.CompilerParams(vmem_limit_bytes=8 << 20),
        name="place",
    )(wire)


def merge_kernel(a, b, c, d, out_t, out_b):
    out_t[...] = (a[...].astype(jnp.float32) + b[...].astype(jnp.float32)).astype(out_t.dtype)
    out_b[...] = (c[...].astype(jnp.float32) + d[...].astype(jnp.float32)).astype(out_b.dtype)


def merge_call(top, passing_t, bottom, passing_b):
    return pl.pallas_call(
        merge_kernel,
        out_shape=[jax.ShapeDtypeStruct(top.shape, top.dtype)] * 2,
        in_specs=[VMEM] * 4,
        out_specs=[VMEM] * 2,
        cost_estimate=pl.CostEstimate(flops=MERGE_FLOPS, bytes_accessed=1 << 18, transcendentals=0),
        name="merge",
    )(top, passing_t, bottom, passing_b)


def finish_kernel(x, *refs):
    *terms, out = refs
    for half in range(2):
        rows = slice(half * HALF, (half + 1) * HALF)
        total = x[rows, :].astype(jnp.float32)
        for term in terms[half::2]:
            total = total + term[...].astype(jnp.float32)
        out[rows, :] = total.astype(out.dtype)


def finish_call(flat, terms):
    return pl.pallas_call(
        finish_kernel,
        out_shape=jax.ShapeDtypeStruct(flat.shape, flat.dtype),
        in_specs=[VMEM] * (1 + len(terms)),
        out_specs=VMEM,
        cost_estimate=pl.CostEstimate(flops=flat.size, bytes_accessed=1 << 18, transcendentals=0),
        name="finish",
    )(flat, *terms)


def swap(x, axis):
    return lax.ppermute(x, axis, [(0, 1), (1, 0)])


def shift(x, by):
    at = lambda z: (z % 2) * (NZ // 2) + z // 2
    return lax.ppermute(x, ("zl", "zh"), [(at(z), at((z + by) % NZ)) for z in range(NZ)])


def on_device(hidden_in, norm_gain, w_q, w_k, w_v, w_o, lengths, dest):
    width = hidden_in.shape[-1]
    per_dev = w_q.shape[1]
    zl, zh, core = lax.axis_index("zl"), lax.axis_index("zh"), lax.axis_index("core")
    meta = jnp.stack([zh * 2 + zl, core]).astype(jnp.int32)
    mine = jnp.concatenate([lengths[0], dest[0, :, 0]])
    theirs = swap(mine, "zl")
    both = jnp.where(zl == 0, jnp.stack([mine, theirs]), jnp.stack([theirs, mine]))
    lens = both[:, :REQ_REP].reshape(-1)
    target = both[:, REQ_REP:]
    same = target[:, :, None] == target[:, None, :]
    earlier = jnp.arange(REQ_REP)[None, :] < jnp.arange(REQ_REP)[:, None]
    rank = jnp.sum((same & earlier[None]).astype(jnp.int32), -1)
    slots = (target // 2) * (2 * CAP) + jnp.arange(2)[:, None] * CAP + rank
    slots = jnp.where(target % 2 == zl, slots, -1).reshape(-1)
    out_rows = lax.axis_size("xy") * 2 * CAP
    empty = 1 - jnp.any(slots[None, :] == jnp.arange(out_rows)[:, None], -1).astype(jnp.int32)

    flat = hidden_in.reshape(ROWS, width)
    bar = lax.optimization_barrier
    tables = (norm_gain.reshape(1, width), *rope_tables(per_dev))
    order, wires = [], []

    def keys(backs, att, keep, key_w, rest_w, chunks, given=()):
        extra, own, other = kv_call(backs, att, keep, meta, lens, tables, key_w, rest_w, chunks, given)
        order.append((backs, 0))
        wires.append(own)
        order.append((backs, 1))
        wires.append(swap(other, "core"))
        return extra, own

    u1, d1 = shift(flat, 1), shift(flat, -1)
    wk_p, wv_p = swap(w_k, "core"), swap(w_v, "core")
    u1, d1, meta, lens, slots, empty, wq_late, wo_late = bar((u1, d1, meta, lens, slots, empty, w_q, w_o))
    u2, d2 = shift(u1, 1), shift(d1, -1)
    rest = (*pinned((w_q,), pltpu.HBM), swap(wq_late, "core"), *pinned((w_o,), pltpu.HBM), swap(wo_late, "core"))
    first = (*pinned((w_k, w_v), pltpu.HBM), wk_p, wv_p)
    (held, *kept), done = keys((0, 1, -1), (), 1, first, (), (*pinned((flat,), pltpu.HBM), u1, d1))
    u2, d2, done = bar((u2, d2, done))
    wires[0] = done
    u3, d3 = shift(u2, 1), shift(d2, -1)
    extra, done = keys((2, -2), (2, -2, 0), 0, (held,), rest, (u2, d2), kept)
    held_rest, (top1, bottom1, top2, bottom2, *part0) = extra[:2], extra[2:]
    u3, d3, done = bar((u3, d3, done))
    wires[2] = done
    far = shift(u3[:HALF], 1), shift(d3[HALF:], -1)
    _, done = keys((3, -3), (), 0, (held,), (), (u3, d3))
    wires[4] = done
    (top3, bottom3), _ = keys((4,), (4,), 0, (held,), held_rest, far)
    passing_t, passing_b = shift(top3, 2), shift(bottom3, -2)
    outbound = pack_call(order, meta, slots, empty, wires)
    inbound = lax.all_to_all(outbound, "xy", split_axis=0, concat_axis=0, tiled=True)
    top1, bottom2, outbound = bar((top1, bottom2, outbound))
    near_t, near_b = shift(top1, -2), shift(bottom2, 2)
    top2, bottom1 = merge_call(top2, passing_t, bottom1, passing_b)
    merged_t, merged_b = shift(top2, 2), shift(bottom1, -2)
    terms = (*part0, near_t, near_b, merged_t, merged_b)
    hidden_out = finish_call(flat, terms).reshape(hidden_in.shape)
    return hidden_out, place_call(inbound, per_dev)


def solution(mesh):
    n_req, n_tp = mesh.devices.shape
    fine = Mesh(mesh.devices.reshape(n_req // 2, 2, n_tp // 2, 2), ("xy", "zl", "zh", "core"))
    req, tp = ("xy", "zl"), ("zh", "core")
    placed = (
        P(req + tp, None, None),
        P(),
        P(None, tp),
        P(None, tp),
        P(None, tp),
        P(tp, None),
        P(req, None),
        P(req, None, None),
    )
    return jax.shard_map(
        on_device,
        mesh=fine,
        in_specs=placed,
        out_specs=(P(req + tp, None, None), P(req, None, None, tp)),
        check_vma=False,
    )
```

```python
import functools

import jax
import jax.numpy as jnp
import numpy as np
from jax import lax
from jax.experimental import pallas as pl
from jax.experimental.pallas import tpu as pltpu
from jax.sharding import Mesh, PartitionSpec as P

HD = 96
CAP = 2
EPS = 1e-05
SLOT = 24
NZ = 8
REQ_REP = 32
REQ_DEV = 4
ROWS = REQ_DEV * SLOT
HALF = ROWS // 2
LANES = 128
MERGE_FLOPS = 3 * 10**10
VMEM = pl.BlockSpec(memory_space=pltpu.VMEM)
SMEM = pl.BlockSpec(memory_space=pltpu.SMEM)
HBM = pl.BlockSpec(memory_space=pltpu.HBM)


def rope_tables(width):
    half = HD // 2
    pos = np.arange(SLOT, dtype=np.float32)
    inv = (np.float32(10000.0) ** (-(np.arange(half, dtype=np.float32) * 2.0) / HD)).astype(np.float32)
    angle = pos[:, None] * inv[None, :]
    cosine = np.tile(np.cos(angle), (1, 2 * (width // HD)))
    sine = np.tile(np.concatenate([-np.sin(angle), np.sin(angle)], 1), (1, width // HD))
    return jnp.asarray(cosine, jnp.float32), jnp.asarray(sine, jnp.float32)


def rotate(x, cosine, sine):
    rows, width = x.shape
    lane = lax.broadcasted_iota(jnp.int32, x.shape, 1) % HD
    ahead = pltpu.roll(x, width - HD // 2, 1)
    behind = pltpu.roll(x, HD // 2, 1)
    turned = jnp.where(lane < HD // 2, ahead, behind)
    reps = rows // SLOT
    return x * jnp.concatenate([cosine] * reps, 0) + turned * jnp.concatenate([sine] * reps, 0)


def first_request(meta, back, other_core=0):
    chip = (meta[0] - back + NZ) % NZ
    core = meta[1] if not other_core else 1 - meta[1]
    return (chip % 2) * REQ_REP + ((chip // 2) * 2 + core) * REQ_DEV


def load(src, dst, sem):
    pltpu.make_async_copy(src, dst, sem).start()


def landed(dst, sem):
    pltpu.make_async_copy(dst, dst, sem).wait()


def columns(shard, size):
    return pl.ds(pl.multiple_of(shard * size, LANES), size)


def tiled(table, rows):
    return jnp.concatenate([table[...]] * (rows // SLOT), 0)


def score_masks(backs, meta, lens, heads):
    row = lax.broadcasted_iota(jnp.int32, (ROWS, ROWS), 0)
    col = lax.broadcasted_iota(jnp.int32, (ROWS, ROWS), 1)
    causal = (row // SLOT == col // SLOT) & (col <= row)
    which = lax.broadcasted_iota(jnp.int32, (1, ROWS), 1) // SLOT
    masks = []
    for back in backs:
        base = first_request(meta, back)
        limit = jnp.zeros((1, ROWS), jnp.int32)
        for j in range(REQ_DEV):
            limit = jnp.where(which == j, lens[base + j] + j * SLOT, limit)
        mask = jnp.where(causal & (col < limit), 1.0, 0.0)
        masks.append(jnp.concatenate([mask] * heads, 0))
    return masks


def attend_shard(shard, masks, x_scr, k_scr, v_scr, wq_scr, cosine, sine, attn_scr):
    n = len(masks)
    per_dev = wq_scr.shape[-1]
    heads = per_dev // HD
    cols = columns(shard, per_dev)
    head = lax.broadcasted_iota(jnp.int32, (ROWS, per_dev), 1) // HD
    q = jnp.dot(x_scr[: n * ROWS, :], wq_scr[shard], preferred_element_type=jnp.float32)
    q = rotate(q, cosine, sine).astype(jnp.bfloat16).astype(jnp.float32)
    for i in range(n):
        at = slice(i * ROWS, (i + 1) * ROWS)
        qi = q[at]
        stacked = jnp.concatenate([jnp.where(head == h, qi, 0.0) for h in range(heads)], 0)
        scores = lax.dot_general(
            stacked.astype(jnp.bfloat16),
            k_scr[at, cols],
            (((1,), (1,)), ((), ())),
            preferred_element_type=jnp.float32,
        ) * np.float32(1.0 / np.sqrt(np.float32(HD)))
        mask = masks[i] > 0.5
        scores = jnp.where(mask, scores, -1e30)
        peak = jnp.max(scores, -1, keepdims=True)
        expo = jnp.where(mask, jnp.exp(scores - peak), 0.0)
        probs = (expo / jnp.sum(expo, -1, keepdims=True)).astype(jnp.bfloat16)
        y = jnp.dot(probs, v_scr[at, cols], preferred_element_type=jnp.float32)
        attn = jnp.where(head == 0, y[:ROWS], 0.0)
        for h in range(1, heads):
            attn = jnp.where(head == h, y[h * ROWS : (h + 1) * ROWS], attn)
        attn_scr[at, cols] = attn.astype(jnp.bfloat16)


def project(attn_scr, wo_scr, part_scr, outs, sems):
    width = wo_scr.shape[1]
    step = 768

    def body(c, carry):
        cols = columns(c, step)
        y = jnp.dot(attn_scr[...], wo_scr[:, cols], preferred_element_type=jnp.float32)
        part_scr[:, cols] = y.astype(jnp.bfloat16)
        return carry

    lax.fori_loop(0, width // step, body, 0)
    for i, out in enumerate(outs):
        load(part_scr.at[pl.ds(i * HALF, HALF)], out, sems.at[i])


def load_keys(weights, wkv_v, sems):
    per_dev = weights[0].shape[1]
    for i, w in enumerate(weights):
        load(w, wkv_v.at[i // 2, :, pl.ds(i % 2 * per_dev, per_dev)], sems.at[i])


def load_rest(weights, wq_v, wo_v, sems):
    wq, wq_p, wo, wo_p = weights
    per_dev = wq.shape[1]
    load(wq, wq_v.at[0], sems.at[0])
    load(wq_p, wq_v.at[1], sems.at[1])
    load(wo, wo_v.at[pl.ds(0, per_dev)], sems.at[2])
    load(wo_p, wo_v.at[pl.ds(per_dev, per_dev)], sems.at[3])


def rest_landed(wo_v, per_dev, sems):
    landed(wo_v.at[pl.ds(0, per_dev)], sems.at[2])
    landed(wo_v.at[pl.ds(per_dev, per_dev)], sems.at[3])


def held_shapes(width, per_dev):
    return [
        pltpu.VMEM((2, width, 2 * per_dev), jnp.bfloat16),
        pltpu.VMEM((2, width, per_dev), jnp.bfloat16),
        pltpu.VMEM((2 * per_dev, width), jnp.bfloat16),
    ]


def pinned(held, space=pltpu.VMEM):
    return [pltpu.with_memory_space_constraint(w, space) for w in held]


def kv_kernel(backs, att, keep, pieces, fill, *refs):
    refs = list(refs)
    take = lambda count: [refs.pop(0) for _ in range(count)]
    fill_keys, fill_rest = fill
    n_att = len(att)
    extra = n_att - len(backs) if n_att else 0
    meta, lens, gain, cosine, sine = take(5)
    key_w = take(4 if fill_keys else 1)
    rest_w = take((4 if fill_rest else 2) if n_att else 0)
    chunks = take(pieces)
    given = take(3 if extra else 0)
    (wkv_v,) = take(1) if fill_keys else key_w
    if n_att:
        wq_v, wo_v = take(2) if fill_rest else rest_w
    parts = take(2 * n_att)
    kept = take(3 if keep else 0)
    wires = take(2)
    g_scr, cos_scr, sin_scr, x_scr, w_scr, wire_scr, small, piece_sem, key_sem, rest_sem, out_sem, given_sem = take(
        12
    )
    if n_att or keep:
        k_scr, v_scr = take(2)
    if n_att:
        attn_scr, part_scr, part_sem = take(3)
    per_dev = wkv_v.shape[2] // 2
    tiles = per_dev // LANES
    rows = len(backs) * ROWS
    load(gain, g_scr, small.at[0])
    spans, at = [], 0
    for i, ref in enumerate(chunks):
        spans.append(pl.ds(at, ref.shape[0]))
        load(ref, x_scr.at[spans[-1]], piece_sem.at[i])
        at += ref.shape[0]
    load(cosine, cos_scr, small.at[1])
    load(sine, sin_scr, small.at[2])
    handed = []
    if extra:
        late = pl.ds(rows, ROWS)
        handed = [x_scr.at[late], k_scr.at[late], v_scr.at[late]]
        for i, (src, dst) in enumerate(zip(given, handed)):
            load(src, dst, given_sem.at[i])
    if fill_keys:
        load_keys(key_w, wkv_v, key_sem)
    if fill_rest:
        load_rest(rest_w, wq_v, wo_v, rest_sem)
    token = lax.broadcasted_iota(jnp.int32, (SLOT, 1), 0)
    alive = []
    for back in backs:
        base = first_request(meta, back)
        for j in range(REQ_DEV):
            alive.append((token < lens[base + j]).astype(jnp.float32))
    alive = jnp.concatenate(alive, 0)
    masks = score_masks(att, meta, lens, per_dev // HD) if n_att else []
    landed(g_scr, small.at[0])
    for i, span in enumerate(spans):
        landed(x_scr.at[span], piece_sem.at[i])
        xf = x_scr[span, :].astype(jnp.float32)
        mean_sq = jnp.mean(xf * xf, -1, keepdims=True)
        x_scr[span, :] = (xf * lax.rsqrt(mean_sq + EPS) * g_scr[...]).astype(jnp.bfloat16)
    landed(cos_scr, small.at[1])
    landed(sin_scr, small.at[2])
    for i, y in enumerate(handed):
        landed(y, given_sem.at[i])
    if keep:
        load(x_scr.at[pl.ds(0, keep * ROWS)], kept[0], small.at[0])

    def body(shard, carry):
        cols = columns(shard, per_dev)
        if fill_keys:
            for i in range(2):
                landed(wkv_v.at[shard, :, pl.ds(i * per_dev, per_dev)], key_sem.at[2 * shard + i])
        y = jnp.dot(x_scr[:rows, :], wkv_v[shard], preferred_element_type=jnp.float32)
        k = rotate(y[:, :per_dev], cos_scr[...], sin_scr[...]).astype(jnp.bfloat16)
        v = y[:, per_dev:].astype(jnp.bfloat16)
        if n_att or keep:
            count = rows if n_att else keep * ROWS
            k_scr[:count, cols] = k[:count]
            v_scr[:count, cols] = v[:count]
        for kv, y in enumerate((k, v)):
            y = jnp.where(alive > 0.5, y.astype(jnp.float32), 0.0)
            for t in range(tiles):
                w_scr[pl.ds(2 * t + kv, rows, stride=2 * tiles), :] = y[:, t * LANES : (t + 1) * LANES]
        wire_scr[shard] = w_scr[...].astype(jnp.bfloat16)
        for i, wire in enumerate(wires):

            @pl.when(shard == i)
            def _():
                load(wire_scr.at[i], wire, out_sem.at[i])

        if fill_rest:
            landed(wq_v.at[shard], rest_sem.at[shard])
        if n_att:
            attend_shard(shard, masks, x_scr, k_scr, v_scr, wq_v, cos_scr[...], sin_scr[...], attn_scr)
        return carry

    lax.fori_loop(0, 2, body, 0)
    if keep:
        load(k_scr, kept[1], small.at[1])
        load(v_scr, kept[2], small.at[2])
    if fill_rest:
        rest_landed(wo_v, per_dev, rest_sem)
    if n_att:
        project(attn_scr, wo_v, part_scr, parts, part_sem)
        for i, part in enumerate(parts):
            landed(part, part_sem.at[i])
    for i, wire in enumerate(wires):
        landed(wire, out_sem.at[i])
    for i, y in enumerate(kept):
        landed(y, small.at[i])


def kv_call(backs, att, keep, meta, lens, tables, key_w, rest_w, chunks, given):
    n = len(backs)
    n_att = len(att)
    fill = (len(key_w) == 4, n_att > 0 and len(rest_w) == 4)
    width, per_dev = key_w[0].shape if fill[0] else (key_w[0].shape[1], key_w[0].shape[2] // 2)
    per_req = SLOT * 2 * per_dev // LANES
    bf16 = lambda *shape: jax.ShapeDtypeStruct(shape, jnp.bfloat16)
    scr = lambda *shape: pltpu.VMEM(shape, jnp.bfloat16)
    held = held_shapes(width, per_dev)
    outs = held[:1] * fill[0] + held[1:] * fill[1]
    n_held = len(outs)
    outs += [bf16(HALF, width)] * (2 * n_att)
    if keep:
        outs += [bf16(keep * ROWS, width)] + [bf16(keep * ROWS, 2 * per_dev)] * 2
    outs += [bf16(n * REQ_DEV * per_req, LANES)] * 2
    dma = pltpu.SemaphoreType.DMA
    scratch = [pltpu.VMEM(y.shape, y.dtype) for y in tables]
    scratch += [
        scr(max(n, n_att) * ROWS, width),
        pltpu.VMEM((n * REQ_DEV * per_req, LANES), jnp.float32),
        scr(2, n * REQ_DEV * per_req, LANES),
        dma((3,)),
        dma((len(chunks),)),
        dma((4,)),
        dma((4,)),
        dma((2,)),
        dma((3,)),
    ]
    local = max(n_att, keep)
    if local:
        scratch += [scr(local * ROWS, 2 * per_dev)] * 2
    if n_att:
        scratch += [scr(n_att * ROWS, 2 * per_dev), scr(n_att * ROWS, width), dma((2 * n_att,))]
    key_w = key_w if fill[0] else pinned(key_w)
    rest_w = rest_w if fill[1] else pinned(rest_w) if n_att else []
    res = pl.pallas_call(
        functools.partial(kv_kernel, backs, att, keep, len(chunks), fill),
        out_shape=outs,
        in_specs=[SMEM, SMEM]
        + [HBM] * 3
        + [HBM if fill[0] else VMEM] * len(key_w)
        + [HBM if fill[1] else VMEM] * len(rest_w)
        + [HBM] * (len(chunks) + len(given)),
        out_specs=[VMEM] * n_held + [HBM] * (len(outs) - n_held),
        scratch_shapes=scratch,
        compiler_params=pltpu.CompilerParams(vmem_limit_bytes=24 << 20),
        cost_estimate=pl.CostEstimate(
            flops=(n + n_att) * ROWS * width * per_dev // 4, bytes_accessed=1 << 18, transcendentals=0
        ),
        name="keys",
    )(meta, lens, *pinned(tables, pltpu.HBM), *key_w, *rest_w, *chunks, *given)
    wire = [r.reshape(n * REQ_DEV, per_req, LANES) for r in res[-2:]]
    return res[:-2], wire[0], wire[1]


def attn_kernel(backs, *refs):
    meta, lens, cosine, sine = refs[:4]
    weights, (x, k, v), (wq_v, wo_v), outs = refs[4:8], refs[8:11], refs[11:13], refs[13:15]
    cos_scr, sin_scr, x_scr, k_scr, v_scr, attn_scr, part_scr, small, rest_sem = refs[15:]
    per_dev = wq_v.shape[2]
    firsts = ((x, x_scr), (cosine, cos_scr), (sine, sin_scr), (k, k_scr), (v, v_scr))
    for i, (src, dst) in enumerate(firsts):
        load(src, dst, small.at[i])
    load_rest(weights, wq_v, wo_v, rest_sem)
    masks = score_masks(backs, meta, lens, per_dev // HD)
    for i, (src, dst) in enumerate(firsts):
        landed(dst, small.at[i])

    def body(shard, carry):
        landed(wq_v.at[shard], rest_sem.at[shard])
        attend_shard(shard, masks, x_scr, k_scr, v_scr, wq_v, cos_scr[...], sin_scr[...], attn_scr)
        return carry

    lax.fori_loop(0, 2, body, 0)
    rest_landed(wo_v, per_dev, rest_sem)
    project(attn_scr, wo_v, part_scr, outs, small)
    for i, out in enumerate(outs):
        landed(out, small.at[i])


def attn_call(backs, meta, lens, tables, weights, kept):
    width, per_dev = weights[0].shape
    scr = lambda *shape: pltpu.VMEM(shape, jnp.bfloat16)
    dma = pltpu.SemaphoreType.DMA
    return pl.pallas_call(
        functools.partial(attn_kernel, backs),
        out_shape=held_shapes(width, per_dev)[1:] + [jax.ShapeDtypeStruct((HALF, width), jnp.bfloat16)] * 2,
        in_specs=[SMEM, SMEM] + [HBM] * 9,
        out_specs=[VMEM] * 2 + [HBM] * 2,
        scratch_shapes=[pltpu.VMEM(y.shape, y.dtype) for y in tables]
        + [scr(*y.shape) for y in kept]
        + [scr(ROWS, 2 * per_dev), scr(ROWS, width)]
        + [dma((5,)), dma((4,))],
        compiler_params=pltpu.CompilerParams(vmem_limit_bytes=24 << 20),
        cost_estimate=pl.CostEstimate(
            flops=ROWS * width * per_dev // 4, bytes_accessed=1 << 18, transcendentals=0
        ),
        name="attend",
    )(meta, lens, *pinned(tables, pltpu.HBM), *weights, *kept)


def pack_kernel(order, meta, slots, empty, *refs):
    sources = refs[: len(order)]
    out, *wires, blank, sem, in_sem = refs[len(order) :]
    for i, (src, dst) in enumerate(zip(sources, wires)):
        load(src, dst, in_sem.at[i])
    blank[...] = jnp.zeros_like(blank)
    for s in range(out.shape[0]):

        @pl.when(empty[s] == 1)
        def _():
            pltpu.make_async_copy(blank, out.at[s], sem).start()

    for w, ((backs, other_core), wire) in enumerate(zip(order, wires)):
        landed(wire, in_sem.at[w])
        for i, back in enumerate(backs):
            base = first_request(meta, back, other_core)
            for j in range(REQ_DEV):
                slot = slots[base + j]

                @pl.when(slot >= 0)
                def _():
                    pltpu.make_async_copy(wire.at[i * REQ_DEV + j], out.at[slot], sem).start()

    pltpu.make_async_copy(out, out, sem).wait()


def pack_call(order, meta, slots, empty, wires):
    per_req = wires[0].shape[1]
    rows = empty.shape[0]
    return pl.pallas_call(
        functools.partial(pack_kernel, order),
        out_shape=pltpu.HBM((rows, per_req, LANES), jnp.bfloat16),
        in_specs=[SMEM] * 3 + [HBM] * len(wires),
        out_specs=HBM,
        scratch_shapes=[pltpu.VMEM(w.shape, w.dtype) for w in wires]
        + [pltpu.VMEM((per_req, LANES), jnp.bfloat16), pltpu.SemaphoreType.DMA]
        + [pltpu.SemaphoreType.DMA((len(wires),))],
        compiler_params=pltpu.CompilerParams(vmem_limit_bytes=24 << 20),
        cost_estimate=pl.CostEstimate(flops=0, bytes_accessed=1 << 18, transcendentals=0),
        name="pack",
    )(meta, slots, empty, *wires)


def place_kernel(wire, out, sem):
    copies = []
    for t in range(wire.shape[2]):
        copies.append(
            pltpu.make_async_copy(wire.at[:, :, t], out.at[:, :, :, pl.ds(t * LANES, LANES)], sem.at[t])
        )
        copies[-1].start()
    for copy in copies:
        copy.wait()


def place_call(inbound, per_dev):
    rows = inbound.shape[0]
    tiles = per_dev // LANES
    wire = inbound.reshape(rows, SLOT, tiles, 2, LANES)
    return pl.pallas_call(
        place_kernel,
        out_shape=jax.ShapeDtypeStruct((rows, SLOT, 2, per_dev), jnp.bfloat16),
        in_specs=[VMEM],
        out_specs=HBM,
        scratch_shapes=[pltpu.SemaphoreType.DMA((tiles,))],
        compiler_params=pltpu.CompilerParams(vmem_limit_bytes=8 << 20),
        name="place",
    )(wire)


def merge_kernel(a, b, c, d, out_t, out_b):
    out_t[...] = (a[...].astype(jnp.float32) + b[...].astype(jnp.float32)).astype(out_t.dtype)
    out_b[...] = (c[...].astype(jnp.float32) + d[...].astype(jnp.float32)).astype(out_b.dtype)


def merge_call(top, passing_t, bottom, passing_b):
    return pl.pallas_call(
        merge_kernel,
        out_shape=[jax.ShapeDtypeStruct(top.shape, top.dtype)] * 2,
        in_specs=[VMEM] * 4,
        out_specs=[VMEM] * 2,
        cost_estimate=pl.CostEstimate(flops=MERGE_FLOPS, bytes_accessed=1 << 18, transcendentals=0),
        name="merge",
    )(top, passing_t, bottom, passing_b)


def finish_kernel(x, *refs):
    *terms, out = refs
    for half in range(2):
        rows = slice(half * HALF, (half + 1) * HALF)
        total = x[rows, :].astype(jnp.float32)
        for term in terms[half::2]:
            total = total + term[...].astype(jnp.float32)
        out[rows, :] = total.astype(out.dtype)


def finish_call(flat, terms):
    rows, width = flat.shape
    step = width // 4
    block = lambda n: pl.BlockSpec((n, step), lambda c: (0, c))
    return pl.pallas_call(
        finish_kernel,
        out_shape=jax.ShapeDtypeStruct(flat.shape, flat.dtype),
        grid=(4,),
        in_specs=[block(rows)] + [block(HALF)] * len(terms),
        out_specs=block(rows),
        cost_estimate=pl.CostEstimate(flops=flat.size, bytes_accessed=1 << 18, transcendentals=0),
        name="finish",
    )(flat, *terms)


def swap(x, axis):
    return lax.ppermute(x, axis, [(0, 1), (1, 0)])


def shift(x, by):
    at = lambda z: (z % 2) * (NZ // 2) + z // 2
    return lax.ppermute(x, ("zl", "zh"), [(at(z), at((z + by) % NZ)) for z in range(NZ)])


def on_device(hidden_in, norm_gain, w_q, w_k, w_v, w_o, lengths, dest):
    width = hidden_in.shape[-1]
    per_dev = w_q.shape[1]
    zl, zh, core = lax.axis_index("zl"), lax.axis_index("zh"), lax.axis_index("core")
    meta = jnp.stack([zh * 2 + zl, core]).astype(jnp.int32)
    mine = jnp.concatenate([lengths[0], dest[0, :, 0]])
    theirs = swap(mine, "zl")
    both = jnp.where(zl == 0, jnp.stack([mine, theirs]), jnp.stack([theirs, mine]))
    lens = both[:, :REQ_REP].reshape(-1)
    target = both[:, REQ_REP:]
    same = target[:, :, None] == target[:, None, :]
    earlier = jnp.arange(REQ_REP)[None, :] < jnp.arange(REQ_REP)[:, None]
    rank = jnp.sum((same & earlier[None]).astype(jnp.int32), -1)
    slots = (target // 2) * (2 * CAP) + jnp.arange(2)[:, None] * CAP + rank
    slots = jnp.where(target % 2 == zl, slots, -1).reshape(-1)
    out_rows = lax.axis_size("xy") * 2 * CAP
    empty = 1 - jnp.any(slots[None, :] == jnp.arange(out_rows)[:, None], -1).astype(jnp.int32)

    flat = hidden_in.reshape(ROWS, width)
    bar = lax.optimization_barrier
    tables = (norm_gain.reshape(1, width), *rope_tables(per_dev))
    order, wires = [], []

    def keys(backs, att, keep, key_w, rest_w, chunks, given=()):
        extra, own, other = kv_call(backs, att, keep, meta, lens, tables, key_w, rest_w, chunks, given)
        order.append((backs, 0))
        wires.append(own)
        order.append((backs, 1))
        wires.append(swap(other, "core"))
        return extra, own

    u1, d1 = shift(flat, 1), shift(flat, -1)
    wk_p, wv_p = swap(w_k, "core"), swap(w_v, "core")
    u1, d1, meta, lens, slots, empty, wq_late, wo_late = bar((u1, d1, meta, lens, slots, empty, w_q, w_o))
    u2, d2 = shift(u1, 1), shift(d1, -1)
    rest = (*pinned((w_q,), pltpu.HBM), swap(wq_late, "core"), *pinned((w_o,), pltpu.HBM), swap(wo_late, "core"))
    first = (*pinned((w_k, w_v), pltpu.HBM), wk_p, wv_p)
    (held, *kept), done = keys((0, 1, -1), (), 1, first, (), (*pinned((flat,), pltpu.HBM), u1, d1))
    *held_rest, top0, bottom0 = attn_call((0,), meta, lens, tables[1:], rest, kept)
    u2, d2, done, top0 = bar((u2, d2, done, top0))
    wires[0] = done
    u3, d3 = shift(u2, 1), shift(d2, -1)
    (top1, bottom1, top2, bottom2), done = keys((2, -2), (2, -2), 0, (held,), held_rest, (u2, d2))
    u3, d3, done = bar((u3, d3, done))
    wires[2] = done
    far = shift(u3[:HALF], 1), shift(d3[HALF:], -1)
    _, done = keys((3, -3), (), 0, (held,), (), (u3, d3))
    wires[4] = done
    (top3, bottom3), _ = keys((4,), (4,), 0, (held,), held_rest, far)
    passing_t, passing_b = shift(top3, 2), shift(bottom3, -2)
    outbound = pack_call(order, meta, slots, empty, wires)
    inbound = lax.all_to_all(outbound, "xy", split_axis=0, concat_axis=0, tiled=True)
    top1, bottom2, outbound = bar((top1, bottom2, outbound))
    near_t, near_b = shift(top1, -2), shift(bottom2, 2)
    top2, bottom1 = merge_call(top2, passing_t, bottom1, passing_b)
    merged_t, merged_b = shift(top2, 2), shift(bottom1, -2)
    terms = (top0, bottom0, near_t, near_b, merged_t, merged_b)
    hidden_out = finish_call(flat, terms).reshape(hidden_in.shape)
    return hidden_out, place_call(inbound, per_dev)


def solution(mesh):
    n_req, n_tp = mesh.devices.shape
    fine = Mesh(mesh.devices.reshape(n_req // 2, 2, n_tp // 2, 2), ("xy", "zl", "zh", "core"))
    req, tp = ("xy", "zl"), ("zh", "core")
    placed = (
        P(req + tp, None, None),
        P(),
        P(None, tp),
        P(None, tp),
        P(None, tp),
        P(tp, None),
        P(req, None),
        P(req, None, None),
    )
    return jax.shard_map(
        on_device,
        mesh=fine,
        in_specs=placed,
        out_specs=(P(req + tp, None, None), P(req, None, None, tp)),
        check_vma=False,
    )
```

```python
import functools

import jax
import jax.numpy as jnp
import numpy as np
from jax import lax
from jax.experimental import pallas as pl
from jax.experimental.pallas import tpu as pltpu
from jax.sharding import Mesh, PartitionSpec as P

HD = 96
CAP = 2
EPS = 1e-05
SLOT = 24
NZ = 8
REQ_REP = 32
REQ_DEV = 4
ROWS = REQ_DEV * SLOT
HALF = ROWS // 2
LANES = 128
MERGE_FLOPS = 3 * 10**10
VMEM = pl.BlockSpec(memory_space=pltpu.VMEM)
SMEM = pl.BlockSpec(memory_space=pltpu.SMEM)
HBM = pl.BlockSpec(memory_space=pltpu.HBM)


def rope_tables(width):
    half = HD // 2
    pos = np.arange(SLOT, dtype=np.float32)
    inv = (np.float32(10000.0) ** (-(np.arange(half, dtype=np.float32) * 2.0) / HD)).astype(np.float32)
    angle = pos[:, None] * inv[None, :]
    cosine = np.tile(np.cos(angle), (1, 2 * (width // HD)))
    sine = np.tile(np.concatenate([-np.sin(angle), np.sin(angle)], 1), (1, width // HD))
    return jnp.asarray(cosine, jnp.float32), jnp.asarray(sine, jnp.float32)


def rotate(x, cosine, sine):
    rows, width = x.shape
    lane = lax.broadcasted_iota(jnp.int32, x.shape, 1) % HD
    ahead = pltpu.roll(x, width - HD // 2, 1)
    behind = pltpu.roll(x, HD // 2, 1)
    turned = jnp.where(lane < HD // 2, ahead, behind)
    reps = rows // SLOT
    return x * jnp.concatenate([cosine] * reps, 0) + turned * jnp.concatenate([sine] * reps, 0)


def first_request(meta, back, other_core=0):
    chip = (meta[0] - back + NZ) % NZ
    core = meta[1] if not other_core else 1 - meta[1]
    return (chip % 2) * REQ_REP + ((chip // 2) * 2 + core) * REQ_DEV


def load(src, dst, sem):
    pltpu.make_async_copy(src, dst, sem).start()


def landed(dst, sem):
    pltpu.make_async_copy(dst, dst, sem).wait()


def columns(shard, size):
    return pl.ds(pl.multiple_of(shard * size, LANES), size)


def tiled(table, rows):
    return jnp.concatenate([table[...]] * (rows // SLOT), 0)


def score_masks(backs, meta, lens, heads):
    row = lax.broadcasted_iota(jnp.int32, (ROWS, ROWS), 0)
    col = lax.broadcasted_iota(jnp.int32, (ROWS, ROWS), 1)
    causal = (row // SLOT == col // SLOT) & (col <= row)
    which = lax.broadcasted_iota(jnp.int32, (1, ROWS), 1) // SLOT
    masks = []
    for back in backs:
        base = first_request(meta, back)
        limit = jnp.zeros((1, ROWS), jnp.int32)
        for j in range(REQ_DEV):
            limit = jnp.where(which == j, lens[base + j] + j * SLOT, limit)
        mask = jnp.where(causal & (col < limit), 1.0, 0.0)
        masks.append(jnp.concatenate([mask] * heads, 0))
    return masks


def attend_shard(shard, masks, x_scr, k_scr, v_scr, wq_scr, cosine, sine, attn_scr):
    n = len(masks)
    per_dev = wq_scr.shape[-1]
    heads = per_dev // HD
    cols = columns(shard, per_dev)
    head = lax.broadcasted_iota(jnp.int32, (ROWS, per_dev), 1) // HD
    q = jnp.dot(x_scr[: n * ROWS, :], wq_scr[shard], preferred_element_type=jnp.float32)
    q = rotate(q, cosine, sine).astype(jnp.bfloat16).astype(jnp.float32)
    for i in range(n):
        at = slice(i * ROWS, (i + 1) * ROWS)
        qi = q[at]
        stacked = jnp.concatenate([jnp.where(head == h, qi, 0.0) for h in range(heads)], 0)
        scores = lax.dot_general(
            stacked.astype(jnp.bfloat16),
            k_scr[at, cols],
            (((1,), (1,)), ((), ())),
            preferred_element_type=jnp.float32,
        ) * np.float32(1.0 / np.sqrt(np.float32(HD)))
        mask = masks[i] > 0.5
        scores = jnp.where(mask, scores, -1e30)
        peak = jnp.max(scores, -1, keepdims=True)
        expo = jnp.where(mask, jnp.exp(scores - peak), 0.0)
        probs = (expo / jnp.sum(expo, -1, keepdims=True)).astype(jnp.bfloat16)
        y = jnp.dot(probs, v_scr[at, cols], preferred_element_type=jnp.float32)
        attn = jnp.where(head == 0, y[:ROWS], 0.0)
        for h in range(1, heads):
            attn = jnp.where(head == h, y[h * ROWS : (h + 1) * ROWS], attn)
        attn_scr[at, cols] = attn.astype(jnp.bfloat16)


def project(attn_scr, wo_scr, part_scr, outs, sems):
    width = wo_scr.shape[1]
    step = 768

    def body(c, carry):
        cols = columns(c, step)
        y = jnp.dot(attn_scr[...], wo_scr[:, cols], preferred_element_type=jnp.float32)
        part_scr[:, cols] = y.astype(jnp.bfloat16)
        return carry

    lax.fori_loop(0, width // step, body, 0)
    for i, out in enumerate(outs):
        load(part_scr.at[pl.ds(i * HALF, HALF)], out, sems.at[i])


def load_keys(weights, wkv_v, sems):
    per_dev = weights[0].shape[1]
    for i, w in enumerate(weights):
        load(w, wkv_v.at[i // 2, :, pl.ds(i % 2 * per_dev, per_dev)], sems.at[i])


def load_rest(weights, wq_v, wo_v, sems):
    wq, wq_p, wo, wo_p = weights
    per_dev = wq.shape[1]
    load(wq, wq_v.at[0], sems.at[0])
    load(wq_p, wq_v.at[1], sems.at[1])
    load(wo, wo_v.at[pl.ds(0, per_dev)], sems.at[2])
    load(wo_p, wo_v.at[pl.ds(per_dev, per_dev)], sems.at[3])


def rest_landed(wo_v, per_dev, sems):
    landed(wo_v.at[pl.ds(0, per_dev)], sems.at[2])
    landed(wo_v.at[pl.ds(per_dev, per_dev)], sems.at[3])


def held_shapes(width, per_dev):
    return [
        pltpu.VMEM((2, width, 2 * per_dev), jnp.bfloat16),
        pltpu.VMEM((2, width, per_dev), jnp.bfloat16),
        pltpu.VMEM((2 * per_dev, width), jnp.bfloat16),
    ]


def pinned(held, space=pltpu.VMEM):
    return [pltpu.with_memory_space_constraint(w, space) for w in held]


def kv_kernel(backs, att, keep, pieces, fill, *refs):
    refs = list(refs)
    take = lambda count: [refs.pop(0) for _ in range(count)]
    fill_keys, fill_rest = fill
    n_att = len(att)
    extra = n_att - len(backs) if n_att else 0
    meta, lens, gain, cosine, sine = take(5)
    key_w = take(4 if fill_keys else 1)
    rest_w = take((4 if fill_rest else 2) if n_att else 0)
    chunks = take(pieces)
    given = take(3 if extra else 0)
    (wkv_v,) = take(1) if fill_keys else key_w
    if n_att:
        wq_v, wo_v = take(2) if fill_rest else rest_w
    parts = take(2 * n_att)
    kept = take(3 if keep else 0)
    wires = take(2)
    g_scr, cos_scr, sin_scr, x_scr, w_scr, wire_scr, small, piece_sem, key_sem, rest_sem, out_sem, given_sem = take(
        12
    )
    if n_att or keep:
        k_scr, v_scr = take(2)
    if n_att:
        attn_scr, part_scr, part_sem = take(3)
    per_dev = wkv_v.shape[2] // 2
    tiles = per_dev // LANES
    rows = len(backs) * ROWS
    load(gain, g_scr, small.at[0])
    spans, at = [], 0
    for i, ref in enumerate(chunks):
        spans.append(pl.ds(at, ref.shape[0]))
        load(ref, x_scr.at[spans[-1]], piece_sem.at[i])
        at += ref.shape[0]
    load(cosine, cos_scr, small.at[1])
    load(sine, sin_scr, small.at[2])
    handed = []
    if extra:
        late = pl.ds(rows, ROWS)
        handed = [x_scr.at[late], k_scr.at[late], v_scr.at[late]]
        for i, (src, dst) in enumerate(zip(given, handed)):
            load(src, dst, given_sem.at[i])
    if fill_keys:
        load_keys(key_w, wkv_v, key_sem)
    if fill_rest:
        load_rest(rest_w, wq_v, wo_v, rest_sem)
    token = lax.broadcasted_iota(jnp.int32, (SLOT, 1), 0)
    alive = []
    for back in backs:
        base = first_request(meta, back)
        for j in range(REQ_DEV):
            alive.append((token < lens[base + j]).astype(jnp.float32))
    alive = jnp.concatenate(alive, 0)
    masks = score_masks(att, meta, lens, per_dev // HD) if n_att else []
    landed(g_scr, small.at[0])
    for i, span in enumerate(spans):
        landed(x_scr.at[span], piece_sem.at[i])
        xf = x_scr[span, :].astype(jnp.float32)
        mean_sq = jnp.mean(xf * xf, -1, keepdims=True)
        x_scr[span, :] = (xf * lax.rsqrt(mean_sq + EPS) * g_scr[...]).astype(jnp.bfloat16)
    landed(cos_scr, small.at[1])
    landed(sin_scr, small.at[2])
    for i, y in enumerate(handed):
        landed(y, given_sem.at[i])
    if keep:
        load(x_scr.at[pl.ds(0, keep * ROWS)], kept[0], small.at[0])

    def body(shard, carry):
        cols = columns(shard, per_dev)
        if fill_keys:
            for i in range(2):
                landed(wkv_v.at[shard, :, pl.ds(i * per_dev, per_dev)], key_sem.at[2 * shard + i])
        y = jnp.dot(x_scr[:rows, :], wkv_v[shard], preferred_element_type=jnp.float32)
        k = rotate(y[:, :per_dev], cos_scr[...], sin_scr[...]).astype(jnp.bfloat16)
        v = y[:, per_dev:].astype(jnp.bfloat16)
        if n_att or keep:
            count = rows if n_att else keep * ROWS
            k_scr[:count, cols] = k[:count]
            v_scr[:count, cols] = v[:count]
        for kv, y in enumerate((k, v)):
            y = jnp.where(alive > 0.5, y.astype(jnp.float32), 0.0)
            for t in range(tiles):
                w_scr[pl.ds(2 * t + kv, rows, stride=2 * tiles), :] = y[:, t * LANES : (t + 1) * LANES]
        wire_scr[shard] = w_scr[...].astype(jnp.bfloat16)
        for i, wire in enumerate(wires):

            @pl.when(shard == i)
            def _():
                load(wire_scr.at[i], wire, out_sem.at[i])

        if fill_rest:
            landed(wq_v.at[shard], rest_sem.at[shard])
        if n_att:
            attend_shard(shard, masks, x_scr, k_scr, v_scr, wq_v, cos_scr[...], sin_scr[...], attn_scr)
        return carry

    lax.fori_loop(0, 2, body, 0)
    if keep:
        load(k_scr, kept[1], small.at[1])
        load(v_scr, kept[2], small.at[2])
    if fill_rest:
        rest_landed(wo_v, per_dev, rest_sem)
    if n_att:
        project(attn_scr, wo_v, part_scr, parts, part_sem)
        for i, part in enumerate(parts):
            landed(part, part_sem.at[i])
    for i, wire in enumerate(wires):
        landed(wire, out_sem.at[i])
    for i, y in enumerate(kept):
        landed(y, small.at[i])


def kv_call(backs, att, keep, meta, lens, tables, key_w, rest_w, chunks, given):
    n = len(backs)
    n_att = len(att)
    fill = (len(key_w) == 4, n_att > 0 and len(rest_w) == 4)
    width, per_dev = key_w[0].shape if fill[0] else (key_w[0].shape[1], key_w[0].shape[2] // 2)
    per_req = SLOT * 2 * per_dev // LANES
    bf16 = lambda *shape: jax.ShapeDtypeStruct(shape, jnp.bfloat16)
    scr = lambda *shape: pltpu.VMEM(shape, jnp.bfloat16)
    held = held_shapes(width, per_dev)
    outs = held[:1] * fill[0] + held[1:] * fill[1]
    n_held = len(outs)
    outs += [bf16(HALF, width)] * (2 * n_att)
    if keep:
        outs += [bf16(keep * ROWS, width)] + [bf16(keep * ROWS, 2 * per_dev)] * 2
    outs += [bf16(n * REQ_DEV * per_req, LANES)] * 2
    dma = pltpu.SemaphoreType.DMA
    scratch = [pltpu.VMEM(y.shape, y.dtype) for y in tables]
    scratch += [
        scr(max(n, n_att) * ROWS, width),
        pltpu.VMEM((n * REQ_DEV * per_req, LANES), jnp.float32),
        scr(2, n * REQ_DEV * per_req, LANES),
        dma((3,)),
        dma((len(chunks),)),
        dma((4,)),
        dma((4,)),
        dma((2,)),
        dma((3,)),
    ]
    local = max(n_att, keep)
    if local:
        scratch += [scr(local * ROWS, 2 * per_dev)] * 2
    if n_att:
        scratch += [scr(n_att * ROWS, 2 * per_dev), scr(n_att * ROWS, width), dma((2 * n_att,))]
    key_w = key_w if fill[0] else pinned(key_w)
    rest_w = rest_w if fill[1] else pinned(rest_w) if n_att else []
    res = pl.pallas_call(
        functools.partial(kv_kernel, backs, att, keep, len(chunks), fill),
        out_shape=outs,
        in_specs=[SMEM, SMEM]
        + [HBM] * 3
        + [HBM if fill[0] else VMEM] * len(key_w)
        + [HBM if fill[1] else VMEM] * len(rest_w)
        + [HBM] * (len(chunks) + len(given)),
        out_specs=[VMEM] * n_held + [HBM] * (len(outs) - n_held),
        scratch_shapes=scratch,
        compiler_params=pltpu.CompilerParams(vmem_limit_bytes=24 << 20),
        cost_estimate=pl.CostEstimate(
            flops=(n + n_att) * ROWS * width * per_dev // 4, bytes_accessed=1 << 18, transcendentals=0
        ),
        name="keys",
    )(meta, lens, *pinned(tables, pltpu.HBM), *key_w, *rest_w, *chunks, *given)
    wire = [r.reshape(n * REQ_DEV, per_req, LANES) for r in res[-2:]]
    return res[:-2], wire[0], wire[1]


def attn_kernel(backs, *refs):
    meta, lens, cosine, sine = refs[:4]
    weights, (x, k, v), (wq_v, wo_v), outs = refs[4:8], refs[8:11], refs[11:13], refs[13:15]
    cos_scr, sin_scr, x_scr, k_scr, v_scr, attn_scr, part_scr, small, rest_sem = refs[15:]
    per_dev = wq_v.shape[2]
    firsts = ((x, x_scr), (cosine, cos_scr), (sine, sin_scr), (k, k_scr), (v, v_scr))
    for i, (src, dst) in enumerate(firsts):
        load(src, dst, small.at[i])
    load_rest(weights, wq_v, wo_v, rest_sem)
    masks = score_masks(backs, meta, lens, per_dev // HD)
    for i, (src, dst) in enumerate(firsts):
        landed(dst, small.at[i])

    def body(shard, carry):
        landed(wq_v.at[shard], rest_sem.at[shard])
        attend_shard(shard, masks, x_scr, k_scr, v_scr, wq_v, cos_scr[...], sin_scr[...], attn_scr)
        return carry

    lax.fori_loop(0, 2, body, 0)
    rest_landed(wo_v, per_dev, rest_sem)
    project(attn_scr, wo_v, part_scr, outs, small)
    for i, out in enumerate(outs):
        landed(out, small.at[i])


def attn_call(backs, meta, lens, tables, weights, kept):
    width, per_dev = weights[0].shape
    scr = lambda *shape: pltpu.VMEM(shape, jnp.bfloat16)
    dma = pltpu.SemaphoreType.DMA
    return pl.pallas_call(
        functools.partial(attn_kernel, backs),
        out_shape=held_shapes(width, per_dev)[1:] + [jax.ShapeDtypeStruct((HALF, width), jnp.bfloat16)] * 2,
        in_specs=[SMEM, SMEM] + [HBM] * 9,
        out_specs=[VMEM] * 2 + [HBM] * 2,
        scratch_shapes=[pltpu.VMEM(y.shape, y.dtype) for y in tables]
        + [scr(*y.shape) for y in kept]
        + [scr(ROWS, 2 * per_dev), scr(ROWS, width)]
        + [dma((5,)), dma((4,))],
        compiler_params=pltpu.CompilerParams(vmem_limit_bytes=24 << 20),
        cost_estimate=pl.CostEstimate(
            flops=ROWS * width * per_dev // 4, bytes_accessed=1 << 18, transcendentals=0
        ),
        name="attend",
    )(meta, lens, *pinned(tables, pltpu.HBM), *weights, *kept)


def pack_kernel(order, meta, slots, empty, *refs):
    sources = refs[: len(order)]
    out, *wires, blank, sem, in_sem = refs[len(order) :]
    for i, (src, dst) in enumerate(zip(sources, wires)):
        load(src, dst, in_sem.at[i])
    blank[...] = jnp.zeros_like(blank)
    for s in range(out.shape[0]):

        @pl.when(empty[s] == 1)
        def _():
            pltpu.make_async_copy(blank, out.at[s], sem).start()

    for w, ((backs, other_core), wire) in enumerate(zip(order, wires)):
        landed(wire, in_sem.at[w])
        for i, back in enumerate(backs):
            base = first_request(meta, back, other_core)
            for j in range(REQ_DEV):
                slot = slots[base + j]

                @pl.when(slot >= 0)
                def _():
                    pltpu.make_async_copy(wire.at[i * REQ_DEV + j], out.at[slot], sem).start()

    pltpu.make_async_copy(out, out, sem).wait()


def pack_call(order, meta, slots, empty, wires):
    per_req = wires[0].shape[1]
    rows = empty.shape[0]
    return pl.pallas_call(
        functools.partial(pack_kernel, order),
        out_shape=pltpu.HBM((rows, per_req, LANES), jnp.bfloat16),
        in_specs=[SMEM] * 3 + [HBM] * len(wires),
        out_specs=HBM,
        scratch_shapes=[pltpu.VMEM(w.shape, w.dtype) for w in wires]
        + [pltpu.VMEM((per_req, LANES), jnp.bfloat16), pltpu.SemaphoreType.DMA]
        + [pltpu.SemaphoreType.DMA((len(wires),))],
        compiler_params=pltpu.CompilerParams(vmem_limit_bytes=24 << 20),
        cost_estimate=pl.CostEstimate(flops=0, bytes_accessed=1 << 18, transcendentals=0),
        name="pack",
    )(meta, slots, empty, *wires)


def place_kernel(wire, out, sem):
    copies = []
    for t in range(wire.shape[2]):
        copies.append(
            pltpu.make_async_copy(wire.at[:, :, t], out.at[:, :, :, pl.ds(t * LANES, LANES)], sem.at[t])
        )
        copies[-1].start()
    for copy in copies:
        copy.wait()


def place_call(inbound, per_dev):
    rows = inbound.shape[0]
    tiles = per_dev // LANES
    wire = inbound.reshape(rows, SLOT, tiles, 2, LANES)
    return pl.pallas_call(
        place_kernel,
        out_shape=jax.ShapeDtypeStruct((rows, SLOT, 2, per_dev), jnp.bfloat16),
        in_specs=[VMEM],
        out_specs=HBM,
        scratch_shapes=[pltpu.SemaphoreType.DMA((tiles,))],
        compiler_params=pltpu.CompilerParams(vmem_limit_bytes=8 << 20),
        name="place",
    )(wire)


def merge_kernel(a, b, c, d, out_t, out_b):
    out_t[...] = (a[...].astype(jnp.float32) + b[...].astype(jnp.float32)).astype(out_t.dtype)
    out_b[...] = (c[...].astype(jnp.float32) + d[...].astype(jnp.float32)).astype(out_b.dtype)


def merge_call(top, passing_t, bottom, passing_b):
    return pl.pallas_call(
        merge_kernel,
        out_shape=[jax.ShapeDtypeStruct(top.shape, top.dtype)] * 2,
        in_specs=[VMEM] * 4,
        out_specs=[VMEM] * 2,
        cost_estimate=pl.CostEstimate(flops=MERGE_FLOPS, bytes_accessed=1 << 18, transcendentals=0),
        name="merge",
    )(top, passing_t, bottom, passing_b)


def finish_kernel(x, *refs):
    *terms, out = refs
    for half in range(2):
        rows = slice(half * HALF, (half + 1) * HALF)
        total = x[rows, :].astype(jnp.float32)
        for term in terms[half::2]:
            total = total + term[...].astype(jnp.float32)
        out[rows, :] = total.astype(out.dtype)


def finish_call(flat, terms):
    return pl.pallas_call(
        finish_kernel,
        out_shape=jax.ShapeDtypeStruct(flat.shape, flat.dtype),
        in_specs=[VMEM] * (1 + len(terms)),
        out_specs=VMEM,
        cost_estimate=pl.CostEstimate(flops=flat.size, bytes_accessed=1 << 18, transcendentals=0),
        name="finish",
    )(flat, *terms)


def swap(x, axis):
    return lax.ppermute(x, axis, [(0, 1), (1, 0)])


def shift(x, by):
    at = lambda z: (z % 2) * (NZ // 2) + z // 2
    return lax.ppermute(x, ("zl", "zh"), [(at(z), at((z + by) % NZ)) for z in range(NZ)])


def on_device(hidden_in, norm_gain, w_q, w_k, w_v, w_o, lengths, dest):
    width = hidden_in.shape[-1]
    per_dev = w_q.shape[1]
    zl, zh, core = lax.axis_index("zl"), lax.axis_index("zh"), lax.axis_index("core")
    meta = jnp.stack([zh * 2 + zl, core]).astype(jnp.int32)
    mine = jnp.concatenate([lengths[0], dest[0, :, 0]])
    theirs = swap(mine, "zl")
    both = jnp.where(zl == 0, jnp.stack([mine, theirs]), jnp.stack([theirs, mine]))
    lens = both[:, :REQ_REP].reshape(-1)
    target = both[:, REQ_REP:]
    same = target[:, :, None] == target[:, None, :]
    earlier = jnp.arange(REQ_REP)[None, :] < jnp.arange(REQ_REP)[:, None]
    rank = jnp.sum((same & earlier[None]).astype(jnp.int32), -1)
    slots = (target // 2) * (2 * CAP) + jnp.arange(2)[:, None] * CAP + rank
    slots = jnp.where(target % 2 == zl, slots, -1).reshape(-1)
    out_rows = lax.axis_size("xy") * 2 * CAP
    empty = 1 - jnp.any(slots[None, :] == jnp.arange(out_rows)[:, None], -1).astype(jnp.int32)

    flat = hidden_in.reshape(ROWS, width)
    bar = lax.optimization_barrier
    tables = (norm_gain.reshape(1, width), *rope_tables(per_dev))
    order, wires = [], []

    def keys(backs, att, keep, key_w, rest_w, chunks, given=()):
        extra, own, other = kv_call(backs, att, keep, meta, lens, tables, key_w, rest_w, chunks, given)
        order.append((backs, 0))
        wires.append(own)
        order.append((backs, 1))
        wires.append(swap(other, "core"))
        return extra, own

    d1 = shift(flat, -1)
    u1 = shift(flat, 1)
    wk_p, wv_p = swap(w_k, "core"), swap(w_v, "core")
    d1, u1, meta, lens, slots, empty, wq_late, wo_late = bar((d1, u1, meta, lens, slots, empty, w_q, w_o))
    u2, d2 = shift(u1, 1), shift(d1, -1)
    rest = (*pinned((w_q,), pltpu.HBM), swap(wq_late, "core"), *pinned((w_o,), pltpu.HBM), swap(wo_late, "core"))
    first = (*pinned((w_k, w_v), pltpu.HBM), wk_p, wv_p)
    (held, *kept), done = keys((0, 1, -1), (), 1, first, (), (*pinned((flat,), pltpu.HBM), u1, d1))
    *held_rest, top0, bottom0 = attn_call((0,), meta, lens, tables[1:], rest, kept)
    u2, d2, done, top0 = bar((u2, d2, done, top0))
    wires[0] = done
    u3, d3 = shift(u2, 1), shift(d2, -1)
    (top1, bottom1, top2, bottom2), done = keys((2, -2), (2, -2), 0, (held,), held_rest, (u2, d2))
    u3, d3, done = bar((u3, d3, done))
    wires[2] = done
    far = shift(u3[:HALF], 1), shift(d3[HALF:], -1)
    _, done = keys((3, -3), (), 0, (held,), (), (u3, d3))
    wires[4] = done
    (top3, bottom3), _ = keys((4,), (4,), 0, (held,), held_rest, far)
    passing_t, passing_b = shift(top3, 2), shift(bottom3, -2)
    outbound = pack_call(order, meta, slots, empty, wires)
    inbound = lax.all_to_all(outbound, "xy", split_axis=0, concat_axis=0, tiled=True)
    top1, bottom2, outbound = bar((top1, bottom2, outbound))
    near_t, near_b = shift(top1, -2), shift(bottom2, 2)
    top2, bottom1 = merge_call(top2, passing_t, bottom1, passing_b)
    merged_t, merged_b = shift(top2, 2), shift(bottom1, -2)
    terms = (top0, bottom0, near_t, near_b, merged_t, merged_b)
    hidden_out = finish_call(flat, terms).reshape(hidden_in.shape)
    return hidden_out, place_call(inbound, per_dev)


def solution(mesh):
    n_req, n_tp = mesh.devices.shape
    fine = Mesh(mesh.devices.reshape(n_req // 2, 2, n_tp // 2, 2), ("xy", "zl", "zh", "core"))
    req, tp = ("xy", "zl"), ("zh", "core")
    placed = (
        P(req + tp, None, None),
        P(),
        P(None, tp),
        P(None, tp),
        P(None, tp),
        P(tp, None),
        P(req, None),
        P(req, None, None),
    )
    return jax.shard_map(
        on_device,
        mesh=fine,
        in_specs=placed,
        out_specs=(P(req + tp, None, None), P(req, None, None, tp)),
        check_vma=False,
    )
```
